32 devices in a mesh: fsdp: 8 (over z, y), tensor: 4 (over x, core).
Axes of the slice: x: 2, y: 2, z: 4, core: 2. Of those that a mesh axis runs over, the one named last changes fastest.
Arguments:
- block_input: bfloat16 [16, 197, 768], P('fsdp'), may hold values from -6 to 6
- output_grad: bfloat16 [16, 197, 768], P('fsdp'), may hold values from -6 to 6
- live_images: int32 [16], P('fsdp'), may hold values from 0 to 1, as said below
- w_qkv: float32 [768, 3, 768], P('fsdp', None, 'tensor'), may hold values from -6 to 6
- w_out: float32 [768, 768], P('tensor', 'fsdp'), may hold values from -0.625 to 0.625
- w_fc1: float32 [768, 3072], P('fsdp', 'tensor'), may hold values from -0.21875 to 0.21875
- w_fc2: float32 [3072, 768], P('tensor', 'fsdp'), may hold values from -0.109375 to 0.109375
- qv_bias: float32 [2, 12, 64], P(None, 'tensor', 'fsdp'), may hold values from -1.2 to 1.2
- fc1_bias: float32 [48, 64], P('tensor', 'fsdp'), may hold values from -1.2 to 1.2
- norm_vec: float32 [6, 768], P(None, 'fsdp'), may hold values from -0.9 to 1.5
- mom_qkv: float32 [2, 768, 3, 768], P(None, 'fsdp', None, 'tensor'), may hold values from -5.0528408 to 5.0528408, as said below
- mom_out: float32 [2, 768, 768], P(None, 'tensor', 'fsdp'), may hold values from -5.0528408 to 5.0528408, as said below
- mom_fc1: float32 [2, 768, 3072], P(None, 'fsdp', 'tensor'), may hold values from -5.0528408 to 5.0528408, as said below
- mom_fc2: float32 [2, 3072, 768], P(None, 'tensor', 'fsdp'), may hold values from -5.0528408 to 5.0528408, as said below
- mom_qvb: float32 [2, 2, 12, 64], P(None, None, 'tensor', 'fsdp'), may hold values from -5.0528408 to 5.0528408, as said below
- mom_fc1b: float32 [2, 48, 64], P(None, 'tensor', 'fsdp'), may hold values from -5.0528408 to 5.0528408, as said below
- mom_vec: float32 [2, 6, 768], P(None, None, 'fsdp'), may hold values from -5.0528408 to 5.0528408, as said below
Outputs:
- block_output: bfloat16 [16, 197, 768], P('fsdp')
- input_grad: float32 [16, 197, 768], P('fsdp')
- grad_qkv: float32 [768, 3, 768], P('fsdp', None, 'tensor')
- grad_out: float32 [768, 768], P('tensor', 'fsdp')
- grad_fc1: float32 [768, 3072], P('fsdp', 'tensor')
- grad_fc2: float32 [3072, 768], P('tensor', 'fsdp')
- grad_qvb: float32 [2, 12, 64], P(None, 'tensor', 'fsdp')
- grad_fc1b: float32 [48, 64], P('tensor', 'fsdp')
- grad_vec: float32 [6, 768], P(None, 'fsdp')
- new_qkv: float32 [768, 3, 768], P('fsdp', None, 'tensor')
- new_out: float32 [768, 768], P('tensor', 'fsdp')
- new_fc1: float32 [768, 3072], P('fsdp', 'tensor')
- new_fc2: float32 [3072, 768], P('tensor', 'fsdp')
- new_qvb: float32 [2, 12, 64], P(None, 'tensor', 'fsdp')
- new_fc1b: float32 [48, 64], P('tensor', 'fsdp')
- new_vec: float32 [6, 768], P(None, 'fsdp')
- newmom_qkv: float32 [2, 768, 3, 768], P(None, 'fsdp', None, 'tensor')
- newmom_out: float32 [2, 768, 768], P(None, 'tensor', 'fsdp')
- newmom_fc1: float32 [2, 768, 3072], P(None, 'fsdp', 'tensor')
- newmom_fc2: float32 [2, 3072, 768], P(None, 'tensor', 'fsdp')
- newmom_qvb: float32 [2, 2, 12, 64], P(None, None, 'tensor', 'fsdp')
- newmom_fc1b: float32 [2, 48, 64], P(None, 'tensor', 'fsdp')
- newmom_vec: float32 [2, 6, 768], P(None, None, 'fsdp')
The draws below stay inside these ranges and needn't reach their ends.
Inputs may be any that keep to these rules, and one draw needn't show every extreme that they name: `live_images`: in each aligned block of 2 slots (those of one index of fsdp) either all images are live or exactly one slot is empty; blocks of both kinds occur in every draw. `mom_qkv`: the second moments are positive. `mom_out`: the second moments are positive. `mom_fc1`: the second moments are positive. `mom_fc2`: the second moments are positive. `mom_qvb`: the second moments are positive. `mom_fc1b`: the second moments are positive. `mom_vec`: the second moments are positive.
All inputs are finite; a program needn't handle non-finite values.
Results may differ from the reference program's by a relative error of at most 0.017.
Values may be sent and summed in bfloat16 or wider, within the bound.
A program may use at most 64 MiB of HBM per device.

```python
import math
import jax
import jax.numpy as jnp
from jax import lax

D = 768
HEADS = 12
HD = 64
FF = 3072
SEQ = 197
SLOTS = 2
IMAGES = 16
TOKENS = 3152
N_FSDP = 8
N_TENSOR = 4


def draw_live_images(key, part):
    devices = IMAGES // SLOTS
    short = jax.random.randint(jax.random.fold_in(key, 11), (devices,), 0, 2)
    short = short.at[0].set(0).at[1].set(1)
    gap = jax.random.randint(jax.random.fold_in(key, 12), (devices,), 0, SLOTS)
    slot_ids = jnp.arange(SLOTS, dtype=jnp.int32)
    empty = (short[:, None] == 1) & (slot_ids[None, :] == gap[:, None])
    return jnp.where(empty, 0, 1).astype(jnp.int32).reshape(IMAGES)


def draw_w_qkv(key, part):
    base = jax.random.truncated_normal(jax.random.fold_in(key, 21), -4.0, 4.0, (D, 3, D), jnp.float32) * D ** (-0.5)
    return base


def draw_norm_vec(key, part):
    gains = jax.random.uniform(jax.random.fold_in(key, 31), (6, D), jnp.float32, 0.5, 1.5)
    shifts = jax.random.truncated_normal(jax.random.fold_in(key, 32), -3.0, 3.0, (6, D), jnp.float32) * 0.3
    row_ids = jnp.arange(6)
    is_gain = (row_ids % 2 == 0) & (row_ids < 4)
    return jnp.where(is_gain[:, None], gains, shifts)


def moment_pair(key, shape, marker):
    own_key = jax.random.fold_in(key, marker)
    first = jax.random.truncated_normal(jax.random.fold_in(own_key, 41), -3.0, 3.0, shape, jnp.float32) * (0.03 * TOKENS ** 0.5)
    spread = jax.random.uniform(jax.random.fold_in(own_key, 42), shape, jnp.float32, math.log(0.3), math.log(3.0))
    second = jnp.exp(spread) * (0.0003 * TOKENS)
    return jnp.stack([first, second])


def draw_mom_qkv(key, part):
    return moment_pair(key, (D, 3, D), 51)


def draw_mom_out(key, part):
    return moment_pair(key, (D, D), 52)


def draw_mom_fc1(key, part):
    return moment_pair(key, (D, FF), 53)


def draw_mom_fc2(key, part):
    return moment_pair(key, (FF, D), 54)


def draw_mom_qvb(key, part):
    return moment_pair(key, (2, HEADS, HD), 55)


def draw_mom_fc1b(key, part):
    return moment_pair(key, (FF // HD, HD), 56)


def draw_mom_vec(key, part):
    return moment_pair(key, (6, D), 57)


def levels(stream_key, dims, shards, low, high):
    level, own = 1.0, jax.random.fold_in(stream_key, 6)
    for dim, blocks in shards:
        draws = jnp.exp(jax.random.uniform(jax.random.fold_in(own, dim), (blocks,), jnp.float32, low / len(shards), high / len(shards)))
        level = level * jnp.repeat(draws, dims[dim] // blocks).reshape([-1 if axis == dim else 1 for axis in range(len(dims))])
    return level


def gaussian(key, dims, scale, limit, split=(), kind=jnp.bfloat16):
    values = scale * jax.random.normal(key, dims, jnp.float32)
    if split:
        values = values * levels(key, dims, split, -0.22, 0.18)
    return jnp.clip(values, -limit, limit).astype(kind)


def setup_inputs(seed: int = 0) -> dict:
    seeds = jax.random.split(jax.random.key(seed), 18)
    block_input = gaussian(seeds[0], (IMAGES, SEQ, D), 1.0, 6.0, ((0, 8),))
    output_grad = gaussian(seeds[1], (IMAGES, SEQ, D), 1.0, 6.0, ((0, 8),))
    live_images = draw_live_images(jax.random.fold_in(seeds[17], 71), 0)
    w_qkv = draw_w_qkv(jax.random.fold_in(seeds[17], 71), 0)
    w_out = gaussian(seeds[4], (D, D), (D // 8) ** -0.5, 0.625, ((0, 4), (1, 8)), jnp.float32)
    w_fc1 = gaussian(seeds[5], (D, FF), D ** -0.5, 0.21875, ((0, 8), (1, 4)), jnp.float32)
    w_fc2 = gaussian(seeds[6], (FF, D), FF ** -0.5, 0.109375, ((0, 4), (1, 8)), jnp.float32)
    qv_bias = gaussian(seeds[7], (2, HEADS, HD), 0.3, 1.2, ((1, 4), (2, 8)), jnp.float32)
    fc1_bias = gaussian(seeds[8], (FF // HD, HD), 0.3, 1.2, ((0, 4), (1, 8)), jnp.float32)
    norm_vec = draw_norm_vec(jax.random.fold_in(seeds[17], 71), 0)
    mom_qkv = draw_mom_qkv(jax.random.fold_in(seeds[17], 71), 0)
    mom_out = draw_mom_out(jax.random.fold_in(seeds[17], 71), 0)
    mom_fc1 = draw_mom_fc1(jax.random.fold_in(seeds[17], 71), 0)
    mom_fc2 = draw_mom_fc2(jax.random.fold_in(seeds[17], 71), 0)
    mom_qvb = draw_mom_qvb(jax.random.fold_in(seeds[17], 71), 0)
    mom_fc1b = draw_mom_fc1b(jax.random.fold_in(seeds[17], 71), 0)
    mom_vec = draw_mom_vec(jax.random.fold_in(seeds[17], 71), 0)
    return dict(block_input=block_input, output_grad=output_grad, live_images=live_images, w_qkv=w_qkv, w_out=w_out, w_fc1=w_fc1, w_fc2=w_fc2, qv_bias=qv_bias, fc1_bias=fc1_bias, norm_vec=norm_vec, mom_qkv=mom_qkv, mom_out=mom_out, mom_fc1=mom_fc1, mom_fc2=mom_fc2, mom_qvb=mom_qvb, mom_fc1b=mom_fc1b, mom_vec=mom_vec)


epsilon = 1e-06
sqrt_half = 0.7071067811865476
inv_root = 0.3989422804014327
corr_one = 1.0 - 0.9 ** 3
corr_two = 1.0 - 0.999 ** 3

def widen_copy(values):
    return lax.optimization_barrier(values.astype(jnp.bfloat16)).astype(jnp.float32)

def norm_forward(values, gain, shift):
    center = values - lax.optimization_barrier(jnp.mean(values, axis=-1, keepdims=True))
    variance = lax.optimization_barrier(jnp.mean(center * center, axis=-1, keepdims=True))
    scale = lax.rsqrt(variance + epsilon)
    normed = center * scale
    return (normed * gain + shift, normed, scale)

def norm_backward(upstream, normed, scale, gain):
    scaled = upstream * gain
    return scale * (scaled - lax.optimization_barrier(jnp.mean(scaled, axis=-1, keepdims=True)) - normed * lax.optimization_barrier(jnp.mean(scaled * normed, axis=-1, keepdims=True)))

def gelu_slope(pre_act):
    return 0.5 * (1.0 + lax.erf(pre_act * sqrt_half)) + pre_act * jnp.exp(-0.5 * pre_act * pre_act) * inv_root

def grouped(left, right, parts):
    count, inner = left.shape
    left_g = left.astype(jnp.float32).reshape(count, parts, inner // parts)
    right_g = right.astype(jnp.float32).reshape(parts, inner // parts, right.shape[1])
    terms = jnp.einsum('ngk,gkm->gnm', left_g, right_g).astype(jnp.bfloat16)
    terms = lax.optimization_barrier(terms)
    return lax.optimization_barrier(jnp.sum(terms.astype(jnp.float32), axis=0))

def grouped_three(upstream, weight, parts):
    count = upstream.shape[0]
    width = weight.shape[0]
    up_g = upstream.astype(jnp.float32).reshape(count, 3, parts, width // parts)
    weight_g = weight.astype(jnp.float32).reshape(width, 3, parts, width // parts)
    terms = jnp.einsum('ncgj,dcgj->gnd', up_g, weight_g).astype(jnp.bfloat16)
    terms = lax.optimization_barrier(terms)
    return lax.optimization_barrier(jnp.sum(terms.astype(jnp.float32), axis=0))

def attend(queries, key_rows, value_rows):
    scores = jnp.einsum('bqhe,bkhe->bhqk', queries.astype(jnp.float32), key_rows.astype(jnp.float32)) * 0.125
    logsum = jax.nn.logsumexp(scores, axis=-1, keepdims=True)
    probs = jnp.exp(scores - logsum).astype(jnp.bfloat16)
    mixed = jnp.einsum('bhqk,bkhe->bqhe', probs.astype(jnp.float32), value_rows.astype(jnp.float32))
    return (mixed.astype(jnp.bfloat16), logsum)

def attend_back(queries, key_rows, value_rows, logsum, upstream):
    qf = queries.astype(jnp.float32)
    kf = key_rows.astype(jnp.float32)
    vf = value_rows.astype(jnp.float32)
    uf = upstream.astype(jnp.float32)
    scores = jnp.einsum('bqhe,bkhe->bhqk', qf, kf) * 0.125
    probs = jnp.exp(scores - logsum)
    probs_low = probs.astype(jnp.bfloat16).astype(jnp.float32)
    dprobs = jnp.einsum('bqhe,bkhe->bhqk', uf, vf)
    dscore = (probs * (dprobs - lax.optimization_barrier(jnp.sum(probs * dprobs, axis=-1, keepdims=True)))).astype(jnp.bfloat16).astype(jnp.float32)
    dquery = 0.125 * jnp.einsum('bhqk,bkhe->bqhe', dscore, kf)
    dkey = 0.125 * jnp.einsum('bhqk,bqhe->bkhe', dscore, qf)
    dvalue = jnp.einsum('bhqk,bqhe->bkhe', probs_low, uf)
    return (dquery, dkey, dvalue)

def adamw(param, grad, moments):
    first = 0.9 * moments[0] + 0.1 * grad
    second = 0.999 * moments[1] + 0.001 * grad * grad
    fresh = param - 0.004 * (first / corr_one / (jnp.sqrt(second / corr_two) + 1e-08) + 0.05 * param)
    return (fresh, jnp.stack([first, second]))

def reference(block_input, output_grad, live_images, w_qkv, w_out, w_fc1, w_fc2, qv_bias, fc1_bias, norm_vec, mom_qkv, mom_out, mom_fc1, mom_fc2, mom_qvb, mom_fc1b, mom_vec):
    low = jnp.bfloat16
    inward = w_qkv.astype(low)
    outward = w_out.astype(low)
    widen = w_fc1.astype(low)
    narrow = w_fc2.astype(low)
    heads_bias = widen_copy(qv_bias).reshape(2, D)
    hidden_bias = widen_copy(fc1_bias).reshape(FF)
    vecf = widen_copy(norm_vec)
    rows = SLOTS * SEQ

    def one_block(carry, item):
        image_rows, grad_rows, live_blk = item
        flat = image_rows.astype(jnp.float32).reshape(rows, D)
        first_norm, unit_one, scale_one = norm_forward(flat, vecf[0], vecf[1])
        normed_one = first_norm.astype(low)
        projected = jnp.einsum('nd,dcj->ncj', normed_one.astype(jnp.float32), inward.astype(jnp.float32))
        shifts = jnp.stack([heads_bias[0], jnp.zeros((D,), jnp.float32), heads_bias[1]])
        triple = (projected + shifts).astype(low).reshape(SLOTS, SEQ, 3, HEADS, HD)
        queries = triple[:, :, 0]
        key_rows = triple[:, :, 1]
        value_rows = triple[:, :, 2]
        mixed, logsum = attend(queries, key_rows, value_rows)
        attn_rows = mixed.reshape(rows, D)
        resid = flat + grouped(attn_rows, outward, N_TENSOR) + vecf[4]
        second_norm, unit_two, scale_two = norm_forward(resid, vecf[2], vecf[3])
        normed_two = second_norm.astype(low)
        pre_act = jnp.dot(normed_two, widen, preferred_element_type=jnp.float32) + hidden_bias
        activ = jax.nn.gelu(pre_act, approximate=False).astype(low)
        mlp_total = grouped(activ, narrow, N_TENSOR)
        row_mask = jnp.broadcast_to(live_blk.astype(jnp.float32)[:, None], (SLOTS, SEQ)).reshape(rows, 1)
        out_rows = (row_mask * (resid + mlp_total + vecf[5])).astype(low)
        grad_flat = grad_rows.astype(jnp.float32).reshape(rows, D) * row_mask
        grad_low = grad_flat.astype(low)
        grad_narrow = jnp.einsum('nf,nd->fd', activ.astype(jnp.float32), grad_low.astype(jnp.float32))
        delta_act = jnp.einsum('nd,fd->nf', grad_low.astype(jnp.float32), narrow.astype(jnp.float32))
        delta_pre = delta_act * gelu_slope(pre_act)
        delta_pre_low = delta_pre.astype(low)
        grad_hidden = lax.optimization_barrier(jnp.sum(delta_pre, axis=0))
        grad_widen = jnp.einsum('nd,nf->df', normed_two.astype(jnp.float32), delta_pre_low.astype(jnp.float32))
        delta_two = grouped(delta_pre_low, widen.T, N_TENSOR)
        delta_resid = grad_flat + norm_backward(delta_two, unit_two, scale_two, vecf[2])
        delta_resid_low = delta_resid.astype(low)
        grad_outward = jnp.einsum('nj,nd->jd', attn_rows.astype(jnp.float32), delta_resid_low.astype(jnp.float32))
        delta_mixed = jnp.einsum('nd,jd->nj', delta_resid_low.astype(jnp.float32), outward.astype(jnp.float32))
        delta_mixed = delta_mixed.astype(low).reshape(SLOTS, SEQ, HEADS, HD)
        delta_query, delta_key, delta_value = attend_back(queries, key_rows, value_rows, logsum, delta_mixed)
        delta_triple = jnp.stack([delta_query, delta_key, delta_value], axis=2).reshape(rows, 3, D)
        grad_heads = jnp.stack([lax.optimization_barrier(jnp.sum(delta_triple[:, 0], axis=0)), lax.optimization_barrier(jnp.sum(delta_triple[:, 2], axis=0))])
        triple_low = delta_triple.astype(low)
        grad_inward = jnp.einsum('nd,ncj->dcj', normed_one.astype(jnp.float32), triple_low.astype(jnp.float32))
        delta_one = grouped_three(triple_low, inward, N_TENSOR)
        in_rows = delta_resid + norm_backward(delta_one, unit_one, scale_one, vecf[0])
        grad_rows_vec = jnp.stack([lax.optimization_barrier(jnp.sum(delta_one * unit_one, axis=0)), lax.optimization_barrier(jnp.sum(delta_one, axis=0)), lax.optimization_barrier(jnp.sum(delta_two * unit_two, axis=0)), lax.optimization_barrier(jnp.sum(delta_two, axis=0)), lax.optimization_barrier(jnp.sum(delta_resid, axis=0)), lax.optimization_barrier(jnp.sum(grad_flat, axis=0))])
        terms = (grad_inward, grad_outward, grad_widen, grad_narrow, grad_heads, grad_hidden, grad_rows_vec)
        carry = tuple((total + term for total, term in zip(carry, terms)))
        return (carry, (out_rows.reshape(SLOTS, SEQ, D), in_rows.reshape(SLOTS, SEQ, D)))
    start = (jnp.zeros((D, 3, D), jnp.float32), jnp.zeros((D, D), jnp.float32), jnp.zeros((D, FF), jnp.float32), jnp.zeros((FF, D), jnp.float32), jnp.zeros((2, D), jnp.float32), jnp.zeros((FF,), jnp.float32), jnp.zeros((6, D), jnp.float32))
    inputs = (block_input.reshape(N_FSDP, SLOTS, SEQ, D), output_grad.reshape(N_FSDP, SLOTS, SEQ, D), live_images.reshape(N_FSDP, SLOTS))
    totals, (outputs, in_grads) = lax.scan(one_block, start, inputs)
    block_output = outputs.reshape(IMAGES, SEQ, D)
    input_grad = in_grads.reshape(IMAGES, SEQ, D)
    grad_qkv, grad_out, grad_fc1, grad_fc2, grad_qvb, grad_fc1b, grad_vec = totals
    grad_qvb = grad_qvb.reshape(2, HEADS, HD)
    grad_fc1b = grad_fc1b.reshape(FF // HD, HD)
    params = (w_qkv, w_out, w_fc1, w_fc2, qv_bias, fc1_bias, norm_vec)
    grads = (grad_qkv, grad_out, grad_fc1, grad_fc2, grad_qvb, grad_fc1b, grad_vec)
    moments = (mom_qkv, mom_out, mom_fc1, mom_fc2, mom_qvb, mom_fc1b, mom_vec)
    stepped = [adamw(param, grad, moment) for param, grad, moment in zip(params, grads, moments)]
    return (block_output, input_grad, grad_qkv, grad_out, grad_fc1, grad_fc2, grad_qvb, grad_fc1b, grad_vec, stepped[0][0], stepped[1][0], stepped[2][0], stepped[3][0], stepped[4][0], stepped[5][0], stepped[6][0], stepped[0][1], stepped[1][1], stepped[2][1], stepped[3][1], stepped[4][1], stepped[5][1], stepped[6][1])
```

```python
import functools

import jax
import jax.numpy as jnp
from jax import lax
from jax.experimental import pallas as pl
from jax.experimental.pallas import tpu as pltpu
from jax.sharding import PartitionSpec as P

HD = 64


epsilon = 1e-06
sqrt_half = 0.7071067811865476
inv_root = 0.3989422804014327
corr_one = 1.0 - 0.9**3
corr_two = 1.0 - 0.999**3


def norm_forward(values, gain, shift):
    center = values - jnp.mean(values, axis=-1, keepdims=True)
    variance = jnp.mean(center * center, axis=-1, keepdims=True)
    scale = lax.rsqrt(variance + epsilon)
    normed = center * scale
    return (normed * gain + shift, normed, scale)


def norm_backward(upstream, normed, scale, gain):
    scaled = upstream * gain
    return scale * (
        scaled
        - jnp.mean(scaled, axis=-1, keepdims=True)
        - normed * jnp.mean(scaled * normed, axis=-1, keepdims=True)
    )


def gelu_slope(pre_act):
    return (
        0.5 * (1.0 + lax.erf(pre_act * sqrt_half))
        + pre_act * jnp.exp(-0.5 * pre_act * pre_act) * inv_root
    )


def attend(queries, key_rows, value_rows):
    scores = (
        jnp.einsum("bqhe,bkhe->bhqk", queries, key_rows, preferred_element_type=jnp.float32) * 0.125
    )
    logsum = jax.nn.logsumexp(scores, axis=-1, keepdims=True)
    probs = jnp.exp(scores - logsum).astype(jnp.bfloat16)
    mixed = jnp.einsum("bhqk,bkhe->bqhe", probs, value_rows, preferred_element_type=jnp.float32)
    return (mixed.astype(jnp.bfloat16), logsum)


def attend_back(queries, key_rows, value_rows, logsum, upstream):
    scores = (
        jnp.einsum("bqhe,bkhe->bhqk", queries, key_rows, preferred_element_type=jnp.float32) * 0.125
    )
    probs = jnp.exp(scores - logsum)
    probs_low = probs.astype(jnp.bfloat16)
    dprobs = jnp.einsum("bqhe,bkhe->bhqk", upstream, value_rows, preferred_element_type=jnp.float32)
    dscore = (probs * (dprobs - jnp.sum(probs * dprobs, axis=-1, keepdims=True))).astype(
        jnp.bfloat16
    )
    dquery = 0.125 * jnp.einsum(
        "bhqk,bkhe->bqhe", dscore, key_rows, preferred_element_type=jnp.float32
    )
    dkey = 0.125 * jnp.einsum(
        "bhqk,bqhe->bkhe", dscore, queries, preferred_element_type=jnp.float32
    )
    dvalue = jnp.einsum("bhqk,bqhe->bkhe", probs_low, upstream, preferred_element_type=jnp.float32)
    return (dquery, dkey, dvalue)


def adamw(param, grad, moments):
    first = 0.9 * moments[0] + 0.1 * grad
    second = 0.999 * moments[1] + 0.001 * grad * grad
    fresh = param - 0.004 * (
        first / corr_one / (jnp.sqrt(second / corr_two) + 1e-08) + 0.05 * param
    )
    return (fresh, jnp.stack([first, second]))


MESH_ID = pl.DeviceIdType.MESH


def exchange(fsdp, tensor, tag, gathers=(), reduces=(), terms=()):
    far_n, across_n = fsdp // 2, tensor // 2
    n_g, n_r, n_t = len(gathers), len(reduces), len(terms)
    low = jnp.bfloat16

    def kernel(*refs):
        refs = list(refs)

        def take(count):
            out, refs[:] = refs[:count], refs[count:]
            return out

        g_in, r_in, t_in = take(n_g), take(n_r), take(n_t)
        g_out, r_out, t_out = take(n_g), take(n_r), take(n_t)
        r_near, r_sum, r_far = take(n_r), take(n_r), take(n_r)
        t_core, t_half, t_across = take(n_t), take(n_t), take(n_t)
        g_send, g_recv, r_send, r_recv, t_send, t_recv = take(6)
        mine = lax.axis_index("fsdp")
        lane = lax.axis_index("tensor")
        far, near = lax.div(mine, 2), lax.rem(mine, 2)
        across, core = lax.div(lane, 2), lax.rem(lane, 2)
        twin = 2 * far + (1 - near)
        mate = 2 * across + (1 - core)

        def ahead(step):
            return lax.rem(far + step, far_n)

        def behind(step):
            return lax.rem(far + far_n - step, far_n)

        barrier = pltpu.get_barrier_semaphore()
        greeted = 0
        if n_g or n_r:
            for who in [twin] + [2 * ahead(j) + near for j in range(1, far_n)]:
                pl.semaphore_signal(barrier, inc=1, device_id=(who, lane), device_id_type=MESH_ID)
                greeted += 1
        if n_t:
            for who in [mate] + [
                2 * lax.rem(across + j, across_n) + core for j in range(1, across_n)
            ]:
                pl.semaphore_signal(barrier, inc=1, device_id=(mine, who), device_id_type=MESH_ID)
                greeted += 1
        pl.semaphore_wait(barrier, greeted)

        def copy(src, dst, send, recv, target):
            return pltpu.make_async_remote_copy(
                src_ref=src,
                dst_ref=dst,
                send_sem=send,
                recv_sem=recv,
                device_id=target,
                device_id_type=MESH_ID,
            )

        def run_gather():
            sent = []
            for j in range(1, far_n):
                for p in range(n_g):
                    sent.append(
                        copy(g_in[p], g_out[p].at[mine], g_send.at[p, j], g_recv.at[p, j],
                             (2 * ahead(j) + near, lane))
                    )
                    sent[-1].start()
            for p in range(n_g):
                sent.append(
                    copy(g_in[p], g_out[p].at[mine], g_send.at[p, far_n], g_recv.at[p, far_n],
                         (twin, lane))
                )
                sent[-1].start()
                g_out[p][mine] = g_in[p][...]
            yield
            for j in range(1, far_n):
                for p in range(n_g):
                    slot = g_out[p].at[2 * behind(j) + near]
                    copy(g_in[p], slot, g_send.at[p, j], g_recv.at[p, j],
                         (2 * ahead(j) + near, lane)).wait_recv()
                    sent.append(
                        copy(slot, slot, g_send.at[p, far_n + j], g_recv.at[p, far_n + j],
                             (twin, lane))
                    )
                    sent[-1].start()
                yield
            for j in range(far_n):
                for p in range(n_g):
                    slot = g_out[p].at[2 * behind(j) + (1 - near)]
                    copy(g_in[p], slot, g_send.at[p, far_n + j], g_recv.at[p, far_n + j],
                         (twin, lane)).wait_recv()
            for entry in sent:
                entry.wait_send()

        def run_reduce():
            order = list(range(1, far_n)) + [0]
            hops = {}
            for p in range(n_r):
                for j in order:
                    hops[p, j] = copy(
                        r_in[p].at[2 * ahead(j) + (1 - near)], r_near[p].at[j],
                        r_send.at[p, j], r_recv.at[p, j], (twin, lane))
                    hops[p, j].start()
            yield
            sent = {}
            for p in range(n_r):
                for j in range(1, far_n):
                    hops[p, j].wait_recv()
                    total = r_in[p][2 * ahead(j) + near].astype(jnp.float32) + r_near[p][j].astype(
                        jnp.float32
                    )
                    r_sum[p][j - 1] = total.astype(r_sum[p].dtype)
                    sent[p, j] = copy(
                        r_sum[p].at[j - 1], r_far[p].at[j - 1],
                        r_send.at[p, far_n + j], r_recv.at[p, far_n + j],
                        (2 * ahead(j) + near, lane))
                    sent[p, j].start()
                    yield
            for p in range(n_r):
                hops[p, 0].wait_recv()
                total = r_in[p][mine].astype(jnp.float32) + r_near[p][0].astype(jnp.float32)
                for j in range(1, far_n):
                    sent[p, j].wait_recv()
                    total = total + r_far[p][j - 1].astype(jnp.float32)
                r_out[p][...] = total
            for entry in list(hops.values()) + list(sent.values()):
                entry.wait_send()

        def run_terms():
            half = [ref.shape[1] // 2 for ref in t_in]
            own = [pl.ds(pl.multiple_of(core * h, h), h) for h in half]
            other = [pl.ds(pl.multiple_of((1 - core) * h, h), h) for h in half]
            first, second, third = {}, {}, {}
            for p in range(n_t):
                first[p] = copy(t_in[p].at[:, other[p]], t_core[p], t_send.at[p, 0],
                                t_recv.at[p, 0], (mine, mate))
                first[p].start()
            yield
            for p in range(n_t):
                first[p].wait_recv()
                t_half[p][...] = (
                    t_in[p][:, own[p]].astype(jnp.float32) + t_core[p][...].astype(jnp.float32)
                ).astype(low)
                for j in range(1, across_n):
                    second[p, j] = copy(
                        t_half[p], t_across[p].at[j - 1], t_send.at[p, 1 + j], t_recv.at[p, 1 + j],
                        (mine, 2 * lax.rem(across + j, across_n) + core))
                    second[p, j].start()
            yield
            yield
            for p in range(n_t):
                total = t_half[p][...].astype(jnp.float32)
                for j in range(1, across_n):
                    second[p, j].wait_recv()
                    total = total + t_across[p][j - 1].astype(jnp.float32)
                t_out[p][:, own[p]] = total.astype(low)
                third[p] = copy(t_out[p].at[:, own[p]], t_out[p].at[:, own[p]], t_send.at[p, 1],
                                t_recv.at[p, 1], (mine, mate))
                third[p].start()
            yield
            for p in range(n_t):
                copy(t_out[p].at[:, own[p]], t_out[p].at[:, other[p]], t_send.at[p, 1],
                     t_recv.at[p, 1], (mine, mate)).wait_recv()
            for entry in list(first.values()) + list(second.values()) + list(third.values()):
                entry.wait_send()

        flows = []
        if n_t:
            flows.append(run_terms())
        if n_g:
            flows.append(run_gather())
        if n_r:
            flows.append(run_reduce())
        while flows:
            for flow in list(flows):
                if next(flow, "end") == "end":
                    flows.remove(flow)

    shape = jax.ShapeDtypeStruct
    outs = (
        [shape((fsdp,) + a.shape, a.dtype) for a in gathers]
        + [shape(a.shape[1:], jnp.float32) for a in reduces]
        + [shape(a.shape, a.dtype) for a in terms]
    )
    few = max(far_n - 1, 1)
    scratch = (
        [pltpu.VMEM((far_n,) + a.shape[1:], a.dtype) for a in reduces]
        + [pltpu.VMEM((few,) + a.shape[1:], a.dtype) for a in reduces]
        + [pltpu.VMEM((few,) + a.shape[1:], a.dtype) for a in reduces]
        + [pltpu.VMEM((a.shape[0], a.shape[1] // 2), low) for a in terms]
        + [pltpu.VMEM((a.shape[0], a.shape[1] // 2), low) for a in terms]
        + [pltpu.VMEM((max(across_n - 1, 1), a.shape[0], a.shape[1] // 2), low) for a in terms]
        + [pltpu.SemaphoreType.DMA((max(n_g, 1), 2 * far_n))] * 2
        + [pltpu.SemaphoreType.DMA((max(n_r, 1), 2 * far_n))] * 2
        + [pltpu.SemaphoreType.DMA((max(n_t, 1), 1 + across_n))] * 2
    )
    args = tuple(gathers) + tuple(reduces) + tuple(terms)
    return pl.pallas_call(
        kernel,
        out_shape=tuple(outs),
        in_specs=[pl.BlockSpec(memory_space=pltpu.VMEM)] * len(args),
        out_specs=tuple([pl.BlockSpec(memory_space=pltpu.VMEM)] * len(outs)),
        scratch_shapes=scratch,
        compiler_params=pltpu.CompilerParams(
            collective_id=tag, has_side_effects=True, vmem_limit_bytes=48 * 1024 * 1024
        ),
        name="exchange_" + str(tag),
    )(*args)


def row_of(values, lanes):
    return jnp.pad(values, [(0, 0)] * (values.ndim - 1) + [(0, lanes - values.shape[-1])])


def plain_step(
    fsdp,
    tensor,
    block_input,
    output_grad,
    live_images,
    w_qkv,
    w_out,
    w_fc1,
    w_fc2,
    qv_bias,
    fc1_bias,
    norm_vec,
    mom_qkv,
    mom_out,
    mom_fc1,
    mom_fc2,
    mom_qvb,
    mom_fc1b,
    mom_vec,
):
    low = jnp.bfloat16
    images, seqlen, width = block_input.shape
    rows = images * seqlen
    owned_rows, _, local_feat = w_qkv.shape
    hidden = w_fc1.shape[1]
    heads_here = local_feat // HD
    n_qvb, n_fc1b = qv_bias.size, fc1_bias.size
    vec_rows = norm_vec.shape[0]
    lanes = -(-max(owned_rows, n_qvb, n_fc1b) // 128) * 128
    small_rows = 16

    small = jnp.concatenate(
        [
            row_of(norm_vec, lanes),
            row_of(fc1_bias.reshape(1, n_fc1b), lanes),
            row_of(qv_bias.reshape(1, n_qvb), lanes),
            jnp.zeros((small_rows - vec_rows - 2, lanes), jnp.float32),
        ]
    ).astype(low)
    small_all, inward, outward = exchange(
        fsdp,
        tensor,
        1,
        gathers=(
            small,
            w_qkv.astype(low).reshape(owned_rows, 3 * local_feat),
            w_out.astype(low).T,
        ),
    )
    inward = inward.reshape(width, 3 * local_feat)
    outward = outward.reshape(width, local_feat)
    smallf = small_all.astype(jnp.float32)
    vecf = smallf[:, :vec_rows, :owned_rows].transpose(1, 0, 2).reshape(vec_rows, width)
    hidden_bias = (
        smallf[:, vec_rows, :n_fc1b]
        .reshape((fsdp,) + fc1_bias.shape)
        .transpose(1, 0, 2)
        .reshape(hidden)
    )
    biasf = (
        smallf[:, vec_rows + 1, :n_qvb]
        .reshape((fsdp,) + qv_bias.shape)
        .transpose(1, 2, 0, 3)
        .reshape(2, local_feat)
    )
    flat = block_input.astype(jnp.float32).reshape(rows, width)
    first_norm, unit_one, scale_one = norm_forward(flat, vecf[0], vecf[1])
    normed_one = first_norm.astype(low)
    shifts = jnp.concatenate([biasf[0], jnp.zeros_like(biasf[0]), biasf[1]])
    projected = jnp.dot(normed_one, inward, preferred_element_type=jnp.float32) + shifts
    triple = projected.astype(low).reshape(images, seqlen, 3, heads_here, HD)
    queries = triple[:, :, 0]
    key_rows = triple[:, :, 1]
    value_rows = triple[:, :, 2]
    mixed, logsum = attend(queries, key_rows, value_rows)
    attn_rows = mixed.reshape(rows, local_feat)
    attn_term = jnp.einsum(
        "nj,dj->nd", attn_rows, outward, preferred_element_type=jnp.float32
    ).astype(low)
    widen, narrow, attn_total = exchange(
        fsdp,
        tensor,
        2,
        gathers=(w_fc1.astype(low), w_fc2.astype(low).T),
        terms=(attn_term,),
    )
    widen = widen.reshape(width, hidden)
    narrow = narrow.reshape(width, hidden)
    resid = flat + attn_total.astype(jnp.float32) + vecf[4]
    second_norm, unit_two, scale_two = norm_forward(resid, vecf[2], vecf[3])
    normed_two = second_norm.astype(low)
    pre_act = jnp.dot(normed_two, widen, preferred_element_type=jnp.float32) + hidden_bias
    activ = jax.nn.gelu(pre_act, approximate=False).astype(low)
    mlp_term = jnp.einsum(
        "nf,df->nd", activ, narrow, preferred_element_type=jnp.float32
    ).astype(low)
    row_mask = jnp.broadcast_to(live_images.astype(jnp.float32)[:, None], (images, seqlen)).reshape(
        rows, 1
    )
    grad_flat = output_grad.astype(jnp.float32).reshape(rows, width) * row_mask
    grad_low = grad_flat.astype(low)
    grad_narrow = jnp.einsum("nd,nf->df", grad_low, activ, preferred_element_type=jnp.float32)
    delta_act = jnp.einsum("nd,df->nf", grad_low, narrow, preferred_element_type=jnp.float32)
    delta_pre = delta_act * gelu_slope(pre_act)
    delta_pre_low = delta_pre.astype(low)
    grad_hidden = jnp.sum(delta_pre, axis=0)
    grad_widen = jnp.einsum(
        "nd,nf->df", normed_two, delta_pre_low, preferred_element_type=jnp.float32
    )
    two_term = jnp.einsum(
        "nf,df->nd", delta_pre_low, widen, preferred_element_type=jnp.float32
    ).astype(low)

    def blocks(grad):
        return grad.astype(low).reshape(fsdp, owned_rows, grad.shape[1])

    own_narrow, own_widen, delta_two, mlp_total = exchange(
        fsdp,
        tensor,
        3,
        reduces=(blocks(grad_narrow), blocks(grad_widen)),
        terms=(two_term, mlp_term),
    )
    delta_two = delta_two.astype(jnp.float32)
    block_output = (
        (row_mask * (resid + mlp_total.astype(jnp.float32) + vecf[5]))
        .astype(low)
        .reshape(images, seqlen, width)
    )
    delta_resid = grad_flat + norm_backward(delta_two, unit_two, scale_two, vecf[2])
    delta_resid_low = delta_resid.astype(low)
    grad_outward = jnp.einsum(
        "nd,nj->dj", delta_resid_low, attn_rows, preferred_element_type=jnp.float32
    )
    delta_mixed = jnp.dot(delta_resid_low, outward, preferred_element_type=jnp.float32)
    delta_mixed = delta_mixed.astype(low).reshape(images, seqlen, heads_here, HD)
    delta_query, delta_key, delta_value = attend_back(
        queries, key_rows, value_rows, logsum, delta_mixed
    )
    delta_triple = jnp.stack([delta_query, delta_key, delta_value], axis=2).reshape(
        rows, 3 * local_feat
    )
    grad_heads = jnp.stack(
        [
            jnp.sum(delta_query, axis=(0, 1)).reshape(local_feat),
            jnp.sum(delta_value, axis=(0, 1)).reshape(local_feat),
        ]
    )
    triple_low = delta_triple.astype(low)
    grad_inward = jnp.einsum(
        "nd,nj->dj", normed_one, triple_low, preferred_element_type=jnp.float32
    )
    one_term = jnp.einsum(
        "nj,dj->nd", triple_low, inward, preferred_element_type=jnp.float32
    ).astype(low)
    own_inward, own_outward, delta_one = exchange(
        fsdp,
        tensor,
        4,
        reduces=(blocks(grad_inward), blocks(grad_outward)),
        terms=(one_term,),
    )
    delta_one = delta_one.astype(jnp.float32)
    input_grad = (delta_resid + norm_backward(delta_one, unit_one, scale_one, vecf[0])).reshape(
        images, seqlen, width
    )
    grad_rows_vec = jnp.stack(
        [
            jnp.sum(delta_one * unit_one, axis=0),
            jnp.sum(delta_one, axis=0),
            jnp.sum(delta_two * unit_two, axis=0),
            jnp.sum(delta_two, axis=0),
            jnp.sum(delta_resid, axis=0),
            jnp.sum(grad_flat, axis=0),
        ]
    )
    r_fc1b, c_fc1b = fc1_bias.shape
    k_qvb, r_qvb, c_qvb = qv_bias.shape
    small_grads = jnp.concatenate(
        [
            row_of(grad_rows_vec.reshape(vec_rows, fsdp, owned_rows).transpose(1, 0, 2), lanes),
            row_of(
                grad_hidden.reshape(r_fc1b, fsdp, c_fc1b).transpose(1, 0, 2).reshape(
                    fsdp, 1, n_fc1b
                ),
                lanes,
            ),
            row_of(
                grad_heads.reshape(k_qvb, r_qvb, fsdp, c_qvb).transpose(2, 0, 1, 3).reshape(
                    fsdp, 1, n_qvb
                ),
                lanes,
            ),
        ],
        axis=1,
    )
    (own_small,) = exchange(fsdp, tensor, 5, reduces=(small_grads,))
    owned = (
        own_inward.reshape(w_qkv.shape),
        own_outward.T,
        own_widen,
        own_narrow.T,
        own_small[vec_rows + 1, :n_qvb].reshape(qv_bias.shape),
        own_small[vec_rows, :n_fc1b].reshape(fc1_bias.shape),
        own_small[:vec_rows, :owned_rows],
    )
    params = (w_qkv, w_out, w_fc1, w_fc2, qv_bias, fc1_bias, norm_vec)
    moments = (mom_qkv, mom_out, mom_fc1, mom_fc2, mom_qvb, mom_fc1b, mom_vec)
    stepped = [adamw(param, grad, moment) for param, grad, moment in zip(params, owned, moments)]
    return (
        (block_output, input_grad)
        + tuple(owned)
        + tuple((entry[0] for entry in stepped))
        + tuple((entry[1] for entry in stepped))
    )


def fused(fsdp, tensor, dims, args):
    images, seqlen, width, owned, feat, hidden, c_fc, c_qv, n_qv = dims
    low, f32 = jnp.bfloat16, jnp.float32
    far_n, across_n = fsdp // 2, tensor // 2
    heads = feat // HD
    padded = args[0].shape[1]
    rows = images * padded
    lanes = args[6].shape[1]
    half = width // 2
    part = owned // 2
    wide = 3 * feat + HD
    combined = 4 * feat
    share = 1.0 / tensor

    def kernel(
        x_ref, gy_ref, wq_ref, wo_ref, w1_ref, w2_ref, small_ref,
        own_g, own_1, own_2, out_ref, in_ref, tot_ref,
        gg, g1, g2, gs, vec, bias, n1, r1, h1, qs, ks, vs, ps, os, x1, n2, r2, h2, slope, us, gfb,
        gx, gxb, gqkv, t_in, t_core, t_half, t_across, t_out,
        rs_in, rs_near, rs_sum, rs_far, sm,
        bsem_s, bsem_r, ysem_s, ysem_r, tsem_s, tsem_r, rsem_s, rsem_r, ssem_s, ssem_r,
    ):
        mine = lax.axis_index("fsdp")
        lane = lax.axis_index("tensor")
        far, near = lax.div(mine, 2), lax.rem(mine, 2)
        across, core = lax.div(lane, 2), lax.rem(lane, 2)
        twin = (2 * far + (1 - near), lane)
        mate = (mine, 2 * across + (1 - core))

        def ahead(step):
            return lax.rem(far + step, far_n)

        def behind(step):
            return lax.rem(far + far_n - step, far_n)

        def other_x(step):
            return (mine, 2 * lax.rem(across + step, across_n) + core)

        barrier = pltpu.get_barrier_semaphore()
        peers = [twin, mate]
        peers += [(2 * ahead(j) + near, lane) for j in range(1, far_n)]
        peers += [other_x(j) for j in range(1, across_n)]
        for who in peers:
            pl.semaphore_signal(barrier, inc=1, device_id=who, device_id_type=MESH_ID)

        def copy(src, dst, send, recv, target):
            return pltpu.make_async_remote_copy(
                src_ref=src, dst_ref=dst, send_sem=send, recv_sem=recv,
                device_id=target, device_id_type=MESH_ID,
            )

        pending = []

        def begin(entry):
            entry.start()
            pending.append(entry)

        gs[mine] = small_ref[...]
        out_t = wo_ref[...].T.astype(low)
        gg[mine] = jnp.concatenate(
            [wq_ref[0].astype(low), wq_ref[1].astype(low), wq_ref[2].astype(low), out_t], axis=1
        )
        g1[mine] = w1_ref[...].astype(low)
        g2[mine] = w2_ref[...].astype(low)
        pl.semaphore_wait(barrier, len(peers))

        units = [(gs, None)]
        for ref in (gg, g1, g2):
            units += [(ref, 0), (ref, 1)]

        def place(u, slot):
            ref, piece = units[u]
            if piece is None:
                return ref.at[slot]
            return ref.at[slot, pl.ds(piece * part, part)]

        def ring(u, s):
            slot = place(u, 2 * behind(s - 1) + near)
            return copy(slot, slot, bsem_s.at[u, s], bsem_r.at[u, s], (2 * ahead(1) + near, lane))

        def ring_wait(u, s):
            slot = place(u, 2 * behind(s) + near)
            copy(slot, slot, bsem_s.at[u, s], bsem_r.at[u, s], (2 * ahead(1) + near, lane)).wait_recv()

        def cross(u, s):
            slot = place(u, 2 * behind(s) + near)
            return copy(slot, slot, ysem_s.at[u, s], ysem_r.at[u, s], twin)

        def cross_wait(u):
            for s in range(far_n):
                slot = place(u, 2 * behind(s) + (1 - near))
                copy(slot, slot, ysem_s.at[u, s], ysem_r.at[u, s], twin).wait_recv()

        groups = [(0, 1, 2), (3, 4), (5, 6)]

        def gather():
            for u in groups[0]:
                begin(ring(u, 1))
                begin(cross(u, 0))
            for index, group in enumerate(groups):
                after = groups[index + 1] if index + 1 < len(groups) else ()
                for s in range(1, far_n):
                    for u in group:
                        yield
                        ring_wait(u, s)
                        if s + 1 < far_n:
                            begin(ring(u, s + 1))
                        begin(cross(u, s))
                    if s + 2 >= far_n and s + 1 < far_n or far_n == 2:
                        for u in after:
                            begin(ring(u, 1))
                for u in after:
                    begin(cross(u, 0))

        flow = gather()

        def step(count=1):
            for _ in range(count):
                next(flow, None)

        step(1)

        for i in range(images):
            xf = x_ref[i].astype(f32)
            center = xf - jnp.mean(xf, axis=-1, keepdims=True)
            scale = lax.rsqrt(jnp.mean(center * center, axis=-1, keepdims=True) + epsilon)
            n1[i] = center * scale
            r1[i] = scale
        per_group = 3 * (far_n - 1)
        step(per_group)
        cross_wait(0)

        def spread(d, carry):
            rows_d = gs[d]
            source = lax.broadcasted_iota(jnp.int32, (lanes, width), 0)
            target = lax.broadcasted_iota(jnp.int32, (lanes, width), 1)
            pick = ((target == d * owned + source) & (source < owned)).astype(f32).astype(low)
            first = jnp.dot(rows_d, pick, preferred_element_type=f32)
            source = lax.broadcasted_iota(jnp.int32, (lanes, hidden), 0)
            target = lax.broadcasted_iota(jnp.int32, (lanes, hidden), 1)
            at = lax.div(source, c_fc) * (c_fc * fsdp) + d * c_fc + lax.rem(source, c_fc)
            pick = ((target == at) & (source * fsdp < hidden)).astype(f32).astype(low)
            second = jnp.dot(rows_d, pick, preferred_element_type=f32)
            source = lax.broadcasted_iota(jnp.int32, (lanes, wide), 0)
            target = lax.broadcasted_iota(jnp.int32, (lanes, wide), 1)
            at = lax.div(source, c_qv) * (c_qv * fsdp) + d * c_qv + lax.rem(source, c_qv)
            at = jnp.where(at < feat, at, at + feat)
            pick = ((target == at) & (source < n_qv)).astype(f32).astype(low)
            third = jnp.dot(rows_d, pick, preferred_element_type=f32)
            return (carry[0] + first, carry[1] + second, carry[2] + third)

        small_rows = small_ref.shape[0]
        start = tuple(jnp.zeros((small_rows, w), f32) for w in (width, hidden, wide))
        spread_v, spread_h, spread_q = lax.fori_loop(0, fsdp, spread, start)
        vec[...] = spread_v
        gain1, shift1, gain2, shift2, bias_o, bias_2 = (vec[r : r + 1] for r in range(6))
        bias_f = spread_h[6:7]
        bias[...] = spread_q[7:8]
        for i in range(images):
            h1[i] = (n1[i] * gain1 + shift1).astype(low)
        cross_wait(1)
        cross_wait(2)

        def flat(ref):
            return ref[...].reshape(ref.shape[0] * ref.shape[1], ref.shape[2])

        def cols(ref, start, size):
            piece = ref[:, :, start : start + size]
            return piece.reshape(ref.shape[0] * ref.shape[1], size)

        span = feat + HD
        k_at, v_at, o_at = feat - HD, 2 * feat, combined - span
        head_of = lax.broadcasted_iota(jnp.int32, (padded, span), 1) // HD
        key_at = lax.broadcasted_iota(jnp.int32, (padded, padded), 1)

        def nn(a, b):
            return jnp.dot(a, b, preferred_element_type=f32)

        def nt(a, b):
            return lax.dot_general(a, b, (((1,), (1,)), ((), ())), preferred_element_type=f32)

        def tn(a, b):
            return lax.dot_general(a, b, (((0,), (0,)), ((), ())), preferred_element_type=f32)

        mine_half = pl.ds(pl.multiple_of(core * half, half), half)
        mate_half = pl.ds(pl.multiple_of((1 - core) * half, half), half)

        def total(k, i):
            def sem(ref, index):
                return ref.at[k, i, index]

            first = copy(t_in.at[k, i, :, mate_half], t_core.at[k, i], sem(tsem_s, 0),
                         sem(tsem_r, 0), mate)
            begin(first)
            yield
            first.wait_recv()
            mine_sum = t_in[k, i, :, mine_half].astype(f32) + t_core[k, i].astype(f32)
            t_half[k, i] = mine_sum.astype(low)
            hops = []
            for j in range(1, across_n):
                hops.append(copy(t_half.at[k, i], t_across.at[k, i, j - 1], sem(tsem_s, 1 + j),
                                 sem(tsem_r, 1 + j), other_x(j)))
                begin(hops[-1])
            yield
            summed = t_half[k, i].astype(f32)
            for j in range(1, across_n):
                hops[j - 1].wait_recv()
                summed = summed + t_across[k, i, j - 1].astype(f32)
            t_out[k, i, :, mine_half] = summed.astype(low)
            own = t_out.at[k, i, :, mine_half]
            begin(copy(own, own, sem(tsem_s, 1), sem(tsem_r, 1), mate))
            yield
            theirs = t_out.at[k, i, :, mate_half]
            copy(theirs, theirs, sem(tsem_s, 1), sem(tsem_r, 1), mate).wait_recv()
            yield

        sums = {}

        def project(i):
            pr = nn(h1[i], cols(gg, 0, wide)) + bias[...]
            qs[i] = pltpu.roll(pr[:, :span], HD, 1).astype(low)
            ks[i] = pr[:, k_at : k_at + span].astype(low)
            vs[i] = pr[:, v_at : v_at + span].astype(low)

        def attend_head(i, h, mixed):
            q_h = jnp.where(head_of == h + 1, qs[i], jnp.zeros_like(qs[i]))
            s = nt(q_h, ks[i]) * 0.125
            s = jnp.where(key_at < seqlen, s, -1e30)
            e = jnp.exp(s - jnp.max(s, axis=-1, keepdims=True))
            p = e * (1.0 / jnp.sum(e, axis=-1, keepdims=True))
            ps[i, h] = p
            o_h = nn(p.astype(low), vs[i])
            return jnp.where(head_of == h, o_h, mixed)

        attn = []
        for i in range(images):
            project(i)
            step(1)
            mixed = jnp.zeros((padded, span), f32)
            for h in range(heads):
                mixed = attend_head(i, h, mixed)
                step(1)
                for entry in attn:
                    if h < 2:
                        next(entry)
            os[i] = pltpu.roll(mixed, HD, 1).astype(low)
            t_in[0, i] = nt(os[i], cols(gg, o_at, span)).astype(low)
            attn.append(total(0, i))
            next(attn[i])
            step(1)
        step(2)
        next(attn[0], None) if images > 1 and heads < 2 else None
        next(attn[-1])
        gy_sum = None
        for i in range(images):
            add = jnp.sum(gy_ref[i].astype(f32), axis=0, keepdims=True)
            gy_sum = add if gy_sum is None else gy_sum + add
        step(1)
        for entry in attn:
            for _ in entry:
                pass
        step(100)

        for i in range(images):
            res = x_ref[i].astype(f32) + t_out[0, i].astype(f32) + bias_o
            x1[i] = res
            center = res - jnp.mean(res, axis=-1, keepdims=True)
            scale = lax.rsqrt(jnp.mean(center * center, axis=-1, keepdims=True) + epsilon)
            unit = center * scale
            n2[i] = unit
            r2[i] = scale
            h2[i] = (unit * gain2 + shift2).astype(low)
        cross_wait(3)
        cross_wait(4)
        for i in range(images):
            f = nn(h2[i], flat(g1)) + bias_f
            phi = 0.5 * (1.0 + lax.erf(f * sqrt_half))
            us[i] = (f * phi).astype(low)
            slope[i] = phi + f * jnp.exp(-0.5 * f * f) * inv_root
        cross_wait(5)
        cross_wait(6)
        two, mlp = [], []
        gf_sum = None
        row2 = row3 = None

        def plus(a, b):
            return b if a is None else a + b

        for i in range(images):
            gf = nn(gy_ref[i], flat(g2)) * slope[i]
            gfb[i] = gf.astype(low)
            gf_sum = plus(gf_sum, jnp.sum(gf, axis=0, keepdims=True))
            t_in[1, i] = nt(gfb[i], flat(g1)).astype(low)
            two.append(total(1, i))
            next(two[i])

        def scatter_y(p):
            for j in list(range(1, far_n)) + [0]:
                begin(copy(rs_in.at[p, 2 * ahead(j) + (1 - near)], rs_near.at[p, j],
                           rsem_s.at[p, j], rsem_r.at[p, j], twin))

        def scatter_z(p, j):
            block = rs_in.at[p, 2 * ahead(j) + (1 - near)]
            copy(block, rs_near.at[p, j], rsem_s.at[p, j], rsem_r.at[p, j], twin).wait_recv()
            rs_sum[p, j - 1] = (
                rs_in[p, 2 * ahead(j) + near].astype(f32) + rs_near[p, j].astype(f32)
            ).astype(low)
            begin(copy(rs_sum.at[p, j - 1], rs_far.at[p, j - 1], rsem_s.at[p, far_n + j],
                       rsem_r.at[p, far_n + j], (2 * ahead(j) + near, lane)))

        def scatter_end(p, ref):
            block = rs_in.at[p, 2 * far + (1 - near)]
            copy(block, rs_near.at[p, 0], rsem_s.at[p, 0], rsem_r.at[p, 0], twin).wait_recv()
            acc = rs_in[p, mine].astype(f32) + rs_near[p, 0].astype(f32)
            for j in range(1, far_n):
                copy(rs_sum.at[p, j - 1], rs_far.at[p, j - 1], rsem_s.at[p, far_n + j],
                     rsem_r.at[p, far_n + j], (2 * ahead(j) + near, lane)).wait_recv()
                acc = acc + rs_far[p, j - 1].astype(f32)
            ref[...] = acc

        def blocks(grad):
            return grad.astype(low).reshape(fsdp, owned, grad.shape[1])

        for i in range(images):
            next(two[i])
        rs_in[0] = blocks(tn(flat(gy_ref), flat(us)))
        rs_in[1] = blocks(tn(flat(h2), flat(gfb)))
        scatter_y(0)
        scatter_y(1)
        for i in range(images):
            t_in[2, i] = nt(us[i], flat(g2)).astype(low)
        for i in range(images):
            term = t_in[1, i].astype(f32)
            row2 = plus(row2, jnp.sum(term * n2[i], axis=0, keepdims=True))
            row3 = plus(row3, jnp.sum(term, axis=0, keepdims=True))
        for i in range(images):
            next(two[i])
        for i in range(images):
            mlp.append(total(2, i))
            next(mlp[i])
        for i in range(images):
            next(two[i])
            next(mlp[i])

        events = [(p, j) for p in range(2) for j in range(1, far_n)]

        def reduce_step():
            if events:
                scatter_z(*events.pop(0))

        gx_sum = row7 = row0 = row1 = None
        one = []
        for i in range(images):
            e = t_out[1, i].astype(f32) * gain2
            unit = n2[i]
            g = gy_ref[i].astype(f32) + r2[i] * (
                e
                - jnp.mean(e, axis=-1, keepdims=True)
                - unit * jnp.mean(e * unit, axis=-1, keepdims=True)
            )
            gx[i] = g
            gxb[i] = g.astype(low)
            gx_sum = plus(gx_sum, jnp.sum(g, axis=0, keepdims=True))
            go = nn(gxb[i], cols(gg, o_at, span))
            go = pltpu.roll(go, span - HD, 1).astype(low)
            dq = jnp.zeros((padded, span), f32)
            dk = jnp.zeros((padded, span), f32)
            dv = jnp.zeros((padded, span), f32)
            for h in range(heads):
                go_h = jnp.where(head_of == h, go, jnp.zeros_like(go))
                p = ps[i, h]
                gp = nt(go_h, vs[i])
                gs_h = (p * (gp - jnp.sum(p * gp, axis=-1, keepdims=True))).astype(low)
                dq = jnp.where(head_of == h + 1, nn(gs_h, ks[i]), dq)
                dk = jnp.where(head_of == h + 1, tn(gs_h, qs[i]), dk)
                dv = jnp.where(head_of == h, tn(p.astype(low), go), dv)
                reduce_step()
            dq = pltpu.roll(dq, span - HD, 1) * 0.125
            dk = dk * 0.125
            edge = 2 * HD
            pieces = jnp.concatenate(
                [dq[:, :edge], dq[:, edge:] + dk[:, :edge], dk[:, edge:], dv], axis=1
            )
            gqkv[i] = pieces.astype(low)
            row7 = plus(row7, jnp.sum(pieces, axis=0, keepdims=True))
            term = nt(gqkv[i], cols(gg, 0, wide)).astype(low)
            t_in[3, i] = term
            one.append(total(3, i))
            next(one[i])
            term = term.astype(f32)
            row0 = plus(row0, jnp.sum(term * n1[i], axis=0, keepdims=True))
            row1 = plus(row1, jnp.sum(term, axis=0, keepdims=True))

        grad = tn(flat(h1), flat(gqkv))
        outer = tn(flat(gxb), flat(os))
        rs_in[2, :, :, :o_at] = blocks(grad[:, :o_at])
        tail = grad[:, o_at:]
        rs_in[2, :, :, o_at : o_at + tail.shape[1]] = blocks(
            tail + outer[:, : tail.shape[1]]
        )
        rs_in[2, :, :, o_at + tail.shape[1] :] = blocks(outer[:, tail.shape[1] :])

        mine_rows = sm.at[0]
        sm[0, 0:1] = row0
        sm[0, 1:2] = row1
        sm[0, 2:3] = row2
        sm[0, 3:4] = row3
        sm[0, 4:5] = gx_sum * share
        sm[0, 5:6] = gy_sum * share
        sm[0, 6:7] = gf_sum
        sm[0, 7:8] = jnp.zeros((1, width), f32)
        sm[0, 7:8, :wide] = row7
        while events:
            reduce_step()
        for i in range(images):
            next(one[i])
        scatter_y(2)
        shared = lax.broadcasted_iota(jnp.int32, (8, width), 0) < 6

        def small_flow():
            hop = copy(sm.at[0], sm.at[1], ssem_s.at[0], ssem_r.at[0], mate)
            begin(hop)
            yield
            hop.wait_recv()
            sm[2] = sm[0] + jnp.where(shared, sm[1], 0.0)
            hops = []
            for j in range(1, across_n):
                hops.append(copy(sm.at[2], sm.at[2 + j], ssem_s.at[j], ssem_r.at[j], other_x(j)))
                begin(hops[-1])
            yield
            summed = sm[2]
            for j in range(1, across_n):
                hops[j - 1].wait_recv()
                summed = summed + jnp.where(shared, sm[2 + j], 0.0)
            base = 2 + across_n
            sm[base] = summed
            hop = copy(sm.at[base], sm.at[base + 1], ssem_s.at[across_n], ssem_r.at[across_n], twin)
            begin(hop)
            yield
            hop.wait_recv()
            sm[base + 2] = sm[base] + sm[base + 1]
            hops = []
            for j in range(1, far_n):
                hops.append(copy(sm.at[base + 2], sm.at[base + 2 + j], ssem_s.at[across_n + j],
                                 ssem_r.at[across_n + j], (2 * ahead(j) + near, lane)))
                begin(hops[-1])
            yield
            summed = sm[base + 2]
            for j in range(1, far_n):
                hops[j - 1].wait_recv()
                summed = summed + sm[base + 2 + j]
            tot_ref[...] = summed
            yield

        tiny = small_flow()
        next(tiny)
        for entry in mlp:
            next(entry)
        next(tiny)
        for i in range(images):
            next(one[i])
        next(tiny)
        scatter_end(0, own_2)
        next(tiny)
        scatter_end(1, own_1)
        for entry in mlp:
            for _ in entry:
                pass
        for i in range(images):
            out_ref[i] = (x1[i] + t_out[2, i].astype(f32) + bias_2).astype(low)
        for j in range(1, far_n):
            scatter_z(2, j)
        next(tiny)
        for i in range(images):
            for _ in one[i]:
                pass
            e = t_out[3, i].astype(f32) * gain1
            unit = n1[i]
            in_ref[i] = gx[i] + r1[i] * (
                e
                - jnp.mean(e, axis=-1, keepdims=True)
                - unit * jnp.mean(e * unit, axis=-1, keepdims=True)
            )
        scatter_end(2, own_g)
        for entry in pending:
            entry.wait_send()

    shape = jax.ShapeDtypeStruct
    outs = (
        shape((owned, combined), f32),
        shape((owned, hidden), f32),
        shape((owned, hidden), f32),
        shape((images, padded, width), low),
        shape((images, padded, width), f32),
        shape((8, width), f32),
    )
    span = feat + HD
    sp = (images, padded)

    def vm(dims, kind):
        return pltpu.VMEM(dims, kind)

    few = max(far_n - 1, 1)
    xs = max(across_n - 1, 1)
    dma = pltpu.SemaphoreType.DMA
    scratch = [
        vm((fsdp, owned, combined), low),
        vm((fsdp, owned, hidden), low),
        vm((fsdp, owned, hidden), low),
        vm((fsdp,) + args[6].shape, low),
        vm((args[6].shape[0], width), f32),
        vm((1, wide), f32),
        vm(sp + (width,), f32), vm(sp + (1,), f32), vm(sp + (width,), low),
        vm(sp + (span,), low), vm(sp + (span,), low), vm(sp + (span,), low),
        vm((images, heads, padded, padded), f32),
        vm(sp + (span,), low),
        vm(sp + (width,), f32),
        vm(sp + (width,), f32), vm(sp + (1,), f32), vm(sp + (width,), low),
        vm(sp + (hidden,), f32), vm(sp + (hidden,), low), vm(sp + (hidden,), low),
        vm(sp + (width,), f32), vm(sp + (width,), low), vm(sp + (wide,), low),
        vm((4,) + sp + (width,), low),
        vm((4,) + sp + (half,), low), vm((4,) + sp + (half,), low),
        vm((4, images, xs, padded, half), low),
        vm((4,) + sp + (width,), low),
        vm((3, fsdp, owned, combined), low),
        vm((3, far_n, owned, combined), low),
        vm((3, few, owned, combined), low),
        vm((3, few, owned, combined), low),
        vm((4 + across_n + far_n, 8, width), f32),
        dma((7, far_n)), dma((7, far_n)), dma((7, far_n)), dma((7, far_n)),
        dma((4, images, 1 + across_n)), dma((4, images, 1 + across_n)),
        dma((3, 2 * far_n)), dma((3, 2 * far_n)),
        dma((across_n + far_n,)), dma((across_n + far_n,)),
    ]
    space = pl.BlockSpec(memory_space=pltpu.VMEM)
    return pl.pallas_call(
        kernel,
        out_shape=outs,
        in_specs=[space] * len(args),
        out_specs=tuple([space] * len(outs)),
        scratch_shapes=scratch,
        compiler_params=pltpu.CompilerParams(
            collective_id=1, has_side_effects=True, vmem_limit_bytes=60 * 1024 * 1024
        ),
        name="fused_layer",
    )(*args)


def update(own, params, moments):
    count = len(own)

    def kernel(*refs):
        g_in, p_in, m_in = refs[:count], refs[count : 2 * count], refs[2 * count : 3 * count]
        p_out, m_out = refs[3 * count : 4 * count], refs[4 * count : 5 * count]
        for g, p, m, np_, nm in zip(g_in, p_in, m_in, p_out, m_out):
            grad, param = g[...], p[...]
            first = 0.9 * m[0] + 0.1 * grad
            second = 0.999 * m[1] + 0.001 * grad * grad
            np_[...] = param - 0.004 * (
                first / corr_one / (jnp.sqrt(second / corr_two) + 1e-08) + 0.05 * param
            )
            nm[0] = first
            nm[1] = second

    shape = jax.ShapeDtypeStruct
    outs = [shape(p.shape, jnp.float32) for p in params]
    outs += [shape(m.shape, jnp.float32) for m in moments]
    space = pl.BlockSpec(memory_space=pltpu.VMEM)
    result = pl.pallas_call(
        kernel,
        out_shape=tuple(outs),
        in_specs=[space] * (3 * count),
        out_specs=tuple([space] * len(outs)),
        compiler_params=pltpu.CompilerParams(vmem_limit_bytes=40 * 1024 * 1024),
        name="update",
    )(*own, *params, *moments)
    return result[:count], result[count:]


def on_device(fsdp, tensor, *args):
    owned = args[3].shape[0]
    local = args[3].shape[2]
    fits = (
        owned % 16 == 0
        and (local + HD) % 128 == 0
        and 4 * local == args[0].shape[2] == args[5].shape[1]
        and fsdp % 2 == 0
        and fsdp <= 16
    )
    return (fused_step if fits else plain_step)(fsdp, tensor, *args)


def fused_step(
    fsdp, tensor, block_input, output_grad, live_images, w_qkv, w_out, w_fc1, w_fc2, qv_bias,
    fc1_bias, norm_vec, mom_qkv, mom_out, mom_fc1, mom_fc2, mom_qvb, mom_fc1b, mom_vec,
):
    low, f32 = jnp.bfloat16, jnp.float32
    images, seqlen, width = block_input.shape
    owned, _, feat = w_qkv.shape
    hidden = w_fc1.shape[1]
    n_qv, n_fc = qv_bias.size, fc1_bias.size
    vec_rows = norm_vec.shape[0]
    lanes = -(-max(owned, n_qv, n_fc) // 128) * 128
    padded = -(-seqlen // 16) * 16
    live = live_images.astype(low)[:, None, None]
    edge = ((0, 0), (0, padded - seqlen), (0, 0))
    x_pad = jnp.pad(block_input, edge)
    gy_pad = jnp.pad(output_grad * live, edge)
    small = jnp.concatenate(
        [
            row_of(norm_vec, lanes),
            row_of(fc1_bias.reshape(1, n_fc), lanes),
            row_of(qv_bias.reshape(1, n_qv), lanes),
            jnp.zeros((16 - vec_rows - 2, lanes), f32),
        ]
    ).astype(low)
    dims = (images, seqlen, width, owned, feat, hidden, fc1_bias.shape[1], qv_bias.shape[2], n_qv)
    wq, w2 = w_qkv.transpose(1, 0, 2), w_fc2.T
    own_g, own_1, own_2, out_rows, in_rows, sums = fused(
        fsdp, tensor, dims, (x_pad, gy_pad, wq, w_out, w_fc1, w2, small)
    )
    block_output = out_rows[:, :seqlen] * live
    input_grad = in_rows[:, :seqlen]
    g_qkv = jnp.stack([own_g[:, c * feat : (c + 1) * feat] for c in range(3)])
    g_out = own_g[:, 3 * feat :].T
    news, moms = update(
        (g_qkv, g_out, own_1, own_2),
        (wq, w_out, w_fc1, w2),
        (mom_qkv.transpose(0, 2, 1, 3), mom_out, mom_fc1, mom_fc2.transpose(0, 2, 1)),
    )
    mine = lax.axis_index("fsdp")
    g_vec = lax.dynamic_slice(sums, (0, mine * owned), (vec_rows, owned))
    r_fc, c_fc = fc1_bias.shape
    g_fc1b = lax.dynamic_slice(
        sums[vec_rows].reshape(r_fc, fsdp * c_fc), (0, mine * c_fc), (r_fc, c_fc)
    )
    k_qv, r_qv, c_qv = qv_bias.shape
    row = sums[vec_rows + 1]
    pair = jnp.stack([row[:feat], row[2 * feat : 3 * feat]]).reshape(k_qv, r_qv, fsdp * c_qv)
    g_qvb = lax.dynamic_slice(pair, (0, 0, mine * c_qv), (k_qv, r_qv, c_qv))
    qvb = adamw(qv_bias, g_qvb, mom_qvb)
    fcb = adamw(fc1_bias, g_fc1b, mom_fc1b)
    nvec = adamw(norm_vec, g_vec, mom_vec)
    return (
        block_output, input_grad,
        g_qkv.transpose(1, 0, 2), g_out, own_1, own_2.T, g_qvb, g_fc1b, g_vec,
        news[0].transpose(1, 0, 2), news[1], news[2], news[3].T, qvb[0], fcb[0], nvec[0],
        moms[0].transpose(0, 2, 1, 3), moms[1], moms[2], moms[3].transpose(0, 2, 1),
        qvb[1], fcb[1], nvec[1],
    )


def solution(mesh):
    return jax.shard_map(
        functools.partial(on_device, mesh.shape["fsdp"], mesh.shape["tensor"]),
        mesh=mesh,
        in_specs=(
            P("fsdp", None, None),
            P("fsdp", None, None),
            P("fsdp"),
            P("fsdp", None, "tensor"),
            P("tensor", "fsdp"),
            P("fsdp", "tensor"),
            P("tensor", "fsdp"),
            P(None, "tensor", "fsdp"),
            P("tensor", "fsdp"),
            P(None, "fsdp"),
            P(None, "fsdp", None, "tensor"),
            P(None, "tensor", "fsdp"),
            P(None, "fsdp", "tensor"),
            P(None, "tensor", "fsdp"),
            P(None, None, "tensor", "fsdp"),
            P(None, "tensor", "fsdp"),
            P(None, None, "fsdp"),
        ),
        out_specs=(
            P("fsdp", None, None),
            P("fsdp", None, None),
            P("fsdp", None, "tensor"),
            P("tensor", "fsdp"),
            P("fsdp", "tensor"),
            P("tensor", "fsdp"),
            P(None, "tensor", "fsdp"),
            P("tensor", "fsdp"),
            P(None, "fsdp"),
            P("fsdp", None, "tensor"),
            P("tensor", "fsdp"),
            P("fsdp", "tensor"),
            P("tensor", "fsdp"),
            P(None, "tensor", "fsdp"),
            P("tensor", "fsdp"),
            P(None, "fsdp"),
            P(None, "fsdp", None, "tensor"),
            P(None, "tensor", "fsdp"),
            P(None, "fsdp", "tensor"),
            P(None, "tensor", "fsdp"),
            P(None, None, "tensor", "fsdp"),
            P(None, "tensor", "fsdp"),
            P(None, None, "fsdp"),
        ),
        check_vma=False,
    )
```

```python
import functools

import jax
import jax.numpy as jnp
from jax import lax
from jax.experimental import pallas as pl
from jax.experimental.pallas import tpu as pltpu
from jax.sharding import PartitionSpec as P

HD = 64


epsilon = 1e-06
sqrt_half = 0.7071067811865476
inv_root = 0.3989422804014327
corr_one = 1.0 - 0.9**3
corr_two = 1.0 - 0.999**3


def norm_forward(values, gain, shift):
    center = values - jnp.mean(values, axis=-1, keepdims=True)
    variance = jnp.mean(center * center, axis=-1, keepdims=True)
    scale = lax.rsqrt(variance + epsilon)
    normed = center * scale
    return (normed * gain + shift, normed, scale)


def norm_backward(upstream, normed, scale, gain):
    scaled = upstream * gain
    return scale * (
        scaled
        - jnp.mean(scaled, axis=-1, keepdims=True)
        - normed * jnp.mean(scaled * normed, axis=-1, keepdims=True)
    )


def gelu_slope(pre_act):
    return (
        0.5 * (1.0 + lax.erf(pre_act * sqrt_half))
        + pre_act * jnp.exp(-0.5 * pre_act * pre_act) * inv_root
    )


def attend(queries, key_rows, value_rows):
    scores = (
        jnp.einsum("bqhe,bkhe->bhqk", queries, key_rows, preferred_element_type=jnp.float32) * 0.125
    )
    logsum = jax.nn.logsumexp(scores, axis=-1, keepdims=True)
    probs = jnp.exp(scores - logsum).astype(jnp.bfloat16)
    mixed = jnp.einsum("bhqk,bkhe->bqhe", probs, value_rows, preferred_element_type=jnp.float32)
    return (mixed.astype(jnp.bfloat16), logsum)


def attend_back(queries, key_rows, value_rows, logsum, upstream):
    scores = (
        jnp.einsum("bqhe,bkhe->bhqk", queries, key_rows, preferred_element_type=jnp.float32) * 0.125
    )
    probs = jnp.exp(scores - logsum)
    probs_low = probs.astype(jnp.bfloat16)
    dprobs = jnp.einsum("bqhe,bkhe->bhqk", upstream, value_rows, preferred_element_type=jnp.float32)
    dscore = (probs * (dprobs - jnp.sum(probs * dprobs, axis=-1, keepdims=True))).astype(
        jnp.bfloat16
    )
    dquery = 0.125 * jnp.einsum(
        "bhqk,bkhe->bqhe", dscore, key_rows, preferred_element_type=jnp.float32
    )
    dkey = 0.125 * jnp.einsum(
        "bhqk,bqhe->bkhe", dscore, queries, preferred_element_type=jnp.float32
    )
    dvalue = jnp.einsum("bhqk,bqhe->bkhe", probs_low, upstream, preferred_element_type=jnp.float32)
    return (dquery, dkey, dvalue)


def adamw(param, grad, moments):
    first = 0.9 * moments[0] + 0.1 * grad
    second = 0.999 * moments[1] + 0.001 * grad * grad
    fresh = param - 0.004 * (
        first / corr_one / (jnp.sqrt(second / corr_two) + 1e-08) + 0.05 * param
    )
    return (fresh, jnp.stack([first, second]))


MESH_ID = pl.DeviceIdType.MESH


def exchange(fsdp, tensor, tag, gathers=(), reduces=(), terms=()):
    far_n, across_n = fsdp // 2, tensor // 2
    n_g, n_r, n_t = len(gathers), len(reduces), len(terms)
    low = jnp.bfloat16

    def kernel(*refs):
        refs = list(refs)

        def take(count):
            out, refs[:] = refs[:count], refs[count:]
            return out

        g_in, r_in, t_in = take(n_g), take(n_r), take(n_t)
        g_out, r_out, t_out = take(n_g), take(n_r), take(n_t)
        r_near, r_sum, r_far = take(n_r), take(n_r), take(n_r)
        t_core, t_half, t_across = take(n_t), take(n_t), take(n_t)
        g_send, g_recv, r_send, r_recv, t_send, t_recv = take(6)
        mine = lax.axis_index("fsdp")
        lane = lax.axis_index("tensor")
        far, near = lax.div(mine, 2), lax.rem(mine, 2)
        across, core = lax.div(lane, 2), lax.rem(lane, 2)
        twin = 2 * far + (1 - near)
        mate = 2 * across + (1 - core)

        def ahead(step):
            return lax.rem(far + step, far_n)

        def behind(step):
            return lax.rem(far + far_n - step, far_n)

        barrier = pltpu.get_barrier_semaphore()
        greeted = 0
        if n_g or n_r:
            for who in [twin] + [2 * ahead(j) + near for j in range(1, far_n)]:
                pl.semaphore_signal(barrier, inc=1, device_id=(who, lane), device_id_type=MESH_ID)
                greeted += 1
        if n_t:
            for who in [mate] + [
                2 * lax.rem(across + j, across_n) + core for j in range(1, across_n)
            ]:
                pl.semaphore_signal(barrier, inc=1, device_id=(mine, who), device_id_type=MESH_ID)
                greeted += 1
        pl.semaphore_wait(barrier, greeted)

        def copy(src, dst, send, recv, target):
            return pltpu.make_async_remote_copy(
                src_ref=src,
                dst_ref=dst,
                send_sem=send,
                recv_sem=recv,
                device_id=target,
                device_id_type=MESH_ID,
            )

        def run_gather():
            sent = []
            for j in range(1, far_n):
                for p in range(n_g):
                    sent.append(
                        copy(g_in[p], g_out[p].at[mine], g_send.at[p, j], g_recv.at[p, j],
                             (2 * ahead(j) + near, lane))
                    )
                    sent[-1].start()
            for p in range(n_g):
                sent.append(
                    copy(g_in[p], g_out[p].at[mine], g_send.at[p, far_n], g_recv.at[p, far_n],
                         (twin, lane))
                )
                sent[-1].start()
                g_out[p][mine] = g_in[p][...]
            yield
            for j in range(1, far_n):
                for p in range(n_g):
                    slot = g_out[p].at[2 * behind(j) + near]
                    copy(g_in[p], slot, g_send.at[p, j], g_recv.at[p, j],
                         (2 * ahead(j) + near, lane)).wait_recv()
                    sent.append(
                        copy(slot, slot, g_send.at[p, far_n + j], g_recv.at[p, far_n + j],
                             (twin, lane))
                    )
                    sent[-1].start()
                yield
            for j in range(far_n):
                for p in range(n_g):
                    slot = g_out[p].at[2 * behind(j) + (1 - near)]
                    copy(g_in[p], slot, g_send.at[p, far_n + j], g_recv.at[p, far_n + j],
                         (twin, lane)).wait_recv()
            for entry in sent:
                entry.wait_send()

        def run_reduce():
            order = list(range(1, far_n)) + [0]
            hops = {}
            for p in range(n_r):
                for j in order:
                    hops[p, j] = copy(
                        r_in[p].at[2 * ahead(j) + (1 - near)], r_near[p].at[j],
                        r_send.at[p, j], r_recv.at[p, j], (twin, lane))
                    hops[p, j].start()
            yield
            sent = {}
            for p in range(n_r):
                for j in range(1, far_n):
                    hops[p, j].wait_recv()
                    total = r_in[p][2 * ahead(j) + near].astype(jnp.float32) + r_near[p][j].astype(
                        jnp.float32
                    )
                    r_sum[p][j - 1] = total.astype(r_sum[p].dtype)
                    sent[p, j] = copy(
                        r_sum[p].at[j - 1], r_far[p].at[j - 1],
                        r_send.at[p, far_n + j], r_recv.at[p, far_n + j],
                        (2 * ahead(j) + near, lane))
                    sent[p, j].start()
                    yield
            for p in range(n_r):
                hops[p, 0].wait_recv()
                total = r_in[p][mine].astype(jnp.float32) + r_near[p][0].astype(jnp.float32)
                for j in range(1, far_n):
                    sent[p, j].wait_recv()
                    total = total + r_far[p][j - 1].astype(jnp.float32)
                r_out[p][...] = total
            for entry in list(hops.values()) + list(sent.values()):
                entry.wait_send()

        def run_terms():
            half = [ref.shape[1] // 2 for ref in t_in]
            own = [pl.ds(pl.multiple_of(core * h, h), h) for h in half]
            other = [pl.ds(pl.multiple_of((1 - core) * h, h), h) for h in half]
            first, second, third = {}, {}, {}
            for p in range(n_t):
                first[p] = copy(t_in[p].at[:, other[p]], t_core[p], t_send.at[p, 0],
                                t_recv.at[p, 0], (mine, mate))
                first[p].start()
            yield
            for p in range(n_t):
                first[p].wait_recv()
                t_half[p][...] = (
                    t_in[p][:, own[p]].astype(jnp.float32) + t_core[p][...].astype(jnp.float32)
                ).astype(low)
                for j in range(1, across_n):
                    second[p, j] = copy(
                        t_half[p], t_across[p].at[j - 1], t_send.at[p, 1 + j], t_recv.at[p, 1 + j],
                        (mine, 2 * lax.rem(across + j, across_n) + core))
                    second[p, j].start()
            yield
            yield
            for p in range(n_t):
                total = t_half[p][...].astype(jnp.float32)
                for j in range(1, across_n):
                    second[p, j].wait_recv()
                    total = total + t_across[p][j - 1].astype(jnp.float32)
                t_out[p][:, own[p]] = total.astype(low)
                third[p] = copy(t_out[p].at[:, own[p]], t_out[p].at[:, own[p]], t_send.at[p, 1],
                                t_recv.at[p, 1], (mine, mate))
                third[p].start()
            yield
            for p in range(n_t):
                copy(t_out[p].at[:, own[p]], t_out[p].at[:, other[p]], t_send.at[p, 1],
                     t_recv.at[p, 1], (mine, mate)).wait_recv()
            for entry in list(first.values()) + list(second.values()) + list(third.values()):
                entry.wait_send()

        flows = []
        if n_t:
            flows.append(run_terms())
        if n_g:
            flows.append(run_gather())
        if n_r:
            flows.append(run_reduce())
        while flows:
            for flow in list(flows):
                if next(flow, "end") == "end":
                    flows.remove(flow)

    shape = jax.ShapeDtypeStruct
    outs = (
        [shape((fsdp,) + a.shape, a.dtype) for a in gathers]
        + [shape(a.shape[1:], jnp.float32) for a in reduces]
        + [shape(a.shape, a.dtype) for a in terms]
    )
    few = max(far_n - 1, 1)
    scratch = (
        [pltpu.VMEM((far_n,) + a.shape[1:], a.dtype) for a in reduces]
        + [pltpu.VMEM((few,) + a.shape[1:], a.dtype) for a in reduces]
        + [pltpu.VMEM((few,) + a.shape[1:], a.dtype) for a in reduces]
        + [pltpu.VMEM((a.shape[0], a.shape[1] // 2), low) for a in terms]
        + [pltpu.VMEM((a.shape[0], a.shape[1] // 2), low) for a in terms]
        + [pltpu.VMEM((max(across_n - 1, 1), a.shape[0], a.shape[1] // 2), low) for a in terms]
        + [pltpu.SemaphoreType.DMA((max(n_g, 1), 2 * far_n))] * 2
        + [pltpu.SemaphoreType.DMA((max(n_r, 1), 2 * far_n))] * 2
        + [pltpu.SemaphoreType.DMA((max(n_t, 1), 1 + across_n))] * 2
    )
    args = tuple(gathers) + tuple(reduces) + tuple(terms)
    return pl.pallas_call(
        kernel,
        out_shape=tuple(outs),
        in_specs=[pl.BlockSpec(memory_space=pltpu.VMEM)] * len(args),
        out_specs=tuple([pl.BlockSpec(memory_space=pltpu.VMEM)] * len(outs)),
        scratch_shapes=scratch,
        compiler_params=pltpu.CompilerParams(
            collective_id=tag, has_side_effects=True, vmem_limit_bytes=48 * 1024 * 1024
        ),
        name="exchange_" + str(tag),
    )(*args)


def row_of(values, lanes):
    return jnp.pad(values, [(0, 0)] * (values.ndim - 1) + [(0, lanes - values.shape[-1])])


def plain_step(
    fsdp,
    tensor,
    block_input,
    output_grad,
    live_images,
    w_qkv,
    w_out,
    w_fc1,
    w_fc2,
    qv_bias,
    fc1_bias,
    norm_vec,
    mom_qkv,
    mom_out,
    mom_fc1,
    mom_fc2,
    mom_qvb,
    mom_fc1b,
    mom_vec,
):
    low = jnp.bfloat16
    images, seqlen, width = block_input.shape
    rows = images * seqlen
    owned_rows, _, local_feat = w_qkv.shape
    hidden = w_fc1.shape[1]
    heads_here = local_feat // HD
    n_qvb, n_fc1b = qv_bias.size, fc1_bias.size
    vec_rows = norm_vec.shape[0]
    lanes = -(-max(owned_rows, n_qvb, n_fc1b) // 128) * 128
    small_rows = 16

    small = jnp.concatenate(
        [
            row_of(norm_vec, lanes),
            row_of(fc1_bias.reshape(1, n_fc1b), lanes),
            row_of(qv_bias.reshape(1, n_qvb), lanes),
            jnp.zeros((small_rows - vec_rows - 2, lanes), jnp.float32),
        ]
    ).astype(low)
    small_all, inward, outward = exchange(
        fsdp,
        tensor,
        1,
        gathers=(
            small,
            w_qkv.astype(low).reshape(owned_rows, 3 * local_feat),
            w_out.astype(low).T,
        ),
    )
    inward = inward.reshape(width, 3 * local_feat)
    outward = outward.reshape(width, local_feat)
    smallf = small_all.astype(jnp.float32)
    vecf = smallf[:, :vec_rows, :owned_rows].transpose(1, 0, 2).reshape(vec_rows, width)
    hidden_bias = (
        smallf[:, vec_rows, :n_fc1b]
        .reshape((fsdp,) + fc1_bias.shape)
        .transpose(1, 0, 2)
        .reshape(hidden)
    )
    biasf = (
        smallf[:, vec_rows + 1, :n_qvb]
        .reshape((fsdp,) + qv_bias.shape)
        .transpose(1, 2, 0, 3)
        .reshape(2, local_feat)
    )
    flat = block_input.astype(jnp.float32).reshape(rows, width)
    first_norm, unit_one, scale_one = norm_forward(flat, vecf[0], vecf[1])
    normed_one = first_norm.astype(low)
    shifts = jnp.concatenate([biasf[0], jnp.zeros_like(biasf[0]), biasf[1]])
    projected = jnp.dot(normed_one, inward, preferred_element_type=jnp.float32) + shifts
    triple = projected.astype(low).reshape(images, seqlen, 3, heads_here, HD)
    queries = triple[:, :, 0]
    key_rows = triple[:, :, 1]
    value_rows = triple[:, :, 2]
    mixed, logsum = attend(queries, key_rows, value_rows)
    attn_rows = mixed.reshape(rows, local_feat)
    attn_term = jnp.einsum(
        "nj,dj->nd", attn_rows, outward, preferred_element_type=jnp.float32
    ).astype(low)
    widen, narrow, attn_total = exchange(
        fsdp,
        tensor,
        2,
        gathers=(w_fc1.astype(low), w_fc2.astype(low).T),
        terms=(attn_term,),
    )
    widen = widen.reshape(width, hidden)
    narrow = narrow.reshape(width, hidden)
    resid = flat + attn_total.astype(jnp.float32) + vecf[4]
    second_norm, unit_two, scale_two = norm_forward(resid, vecf[2], vecf[3])
    normed_two = second_norm.astype(low)
    pre_act = jnp.dot(normed_two, widen, preferred_element_type=jnp.float32) + hidden_bias
    activ = jax.nn.gelu(pre_act, approximate=False).astype(low)
    mlp_term = jnp.einsum(
        "nf,df->nd", activ, narrow, preferred_element_type=jnp.float32
    ).astype(low)
    row_mask = jnp.broadcast_to(live_images.astype(jnp.float32)[:, None], (images, seqlen)).reshape(
        rows, 1
    )
    grad_flat = output_grad.astype(jnp.float32).reshape(rows, width) * row_mask
    grad_low = grad_flat.astype(low)
    grad_narrow = jnp.einsum("nd,nf->df", grad_low, activ, preferred_element_type=jnp.float32)
    delta_act = jnp.einsum("nd,df->nf", grad_low, narrow, preferred_element_type=jnp.float32)
    delta_pre = delta_act * gelu_slope(pre_act)
    delta_pre_low = delta_pre.astype(low)
    grad_hidden = jnp.sum(delta_pre, axis=0)
    grad_widen = jnp.einsum(
        "nd,nf->df", normed_two, delta_pre_low, preferred_element_type=jnp.float32
    )
    two_term = jnp.einsum(
        "nf,df->nd", delta_pre_low, widen, preferred_element_type=jnp.float32
    ).astype(low)

    def blocks(grad):
        return grad.astype(low).reshape(fsdp, owned_rows, grad.shape[1])

    own_narrow, own_widen, delta_two, mlp_total = exchange(
        fsdp,
        tensor,
        3,
        reduces=(blocks(grad_narrow), blocks(grad_widen)),
        terms=(two_term, mlp_term),
    )
    delta_two = delta_two.astype(jnp.float32)
    block_output = (
        (row_mask * (resid + mlp_total.astype(jnp.float32) + vecf[5]))
        .astype(low)
        .reshape(images, seqlen, width)
    )
    delta_resid = grad_flat + norm_backward(delta_two, unit_two, scale_two, vecf[2])
    delta_resid_low = delta_resid.astype(low)
    grad_outward = jnp.einsum(
        "nd,nj->dj", delta_resid_low, attn_rows, preferred_element_type=jnp.float32
    )
    delta_mixed = jnp.dot(delta_resid_low, outward, preferred_element_type=jnp.float32)
    delta_mixed = delta_mixed.astype(low).reshape(images, seqlen, heads_here, HD)
    delta_query, delta_key, delta_value = attend_back(
        queries, key_rows, value_rows, logsum, delta_mixed
    )
    delta_triple = jnp.stack([delta_query, delta_key, delta_value], axis=2).reshape(
        rows, 3 * local_feat
    )
    grad_heads = jnp.stack(
        [
            jnp.sum(delta_query, axis=(0, 1)).reshape(local_feat),
            jnp.sum(delta_value, axis=(0, 1)).reshape(local_feat),
        ]
    )
    triple_low = delta_triple.astype(low)
    grad_inward = jnp.einsum(
        "nd,nj->dj", normed_one, triple_low, preferred_element_type=jnp.float32
    )
    one_term = jnp.einsum(
        "nj,dj->nd", triple_low, inward, preferred_element_type=jnp.float32
    ).astype(low)
    own_inward, own_outward, delta_one = exchange(
        fsdp,
        tensor,
        4,
        reduces=(blocks(grad_inward), blocks(grad_outward)),
        terms=(one_term,),
    )
    delta_one = delta_one.astype(jnp.float32)
    input_grad = (delta_resid + norm_backward(delta_one, unit_one, scale_one, vecf[0])).reshape(
        images, seqlen, width
    )
    grad_rows_vec = jnp.stack(
        [
            jnp.sum(delta_one * unit_one, axis=0),
            jnp.sum(delta_one, axis=0),
            jnp.sum(delta_two * unit_two, axis=0),
            jnp.sum(delta_two, axis=0),
            jnp.sum(delta_resid, axis=0),
            jnp.sum(grad_flat, axis=0),
        ]
    )
    r_fc1b, c_fc1b = fc1_bias.shape
    k_qvb, r_qvb, c_qvb = qv_bias.shape
    small_grads = jnp.concatenate(
        [
            row_of(grad_rows_vec.reshape(vec_rows, fsdp, owned_rows).transpose(1, 0, 2), lanes),
            row_of(
                grad_hidden.reshape(r_fc1b, fsdp, c_fc1b).transpose(1, 0, 2).reshape(
                    fsdp, 1, n_fc1b
                ),
                lanes,
            ),
            row_of(
                grad_heads.reshape(k_qvb, r_qvb, fsdp, c_qvb).transpose(2, 0, 1, 3).reshape(
                    fsdp, 1, n_qvb
                ),
                lanes,
            ),
        ],
        axis=1,
    )
    (own_small,) = exchange(fsdp, tensor, 5, reduces=(small_grads,))
    owned = (
        own_inward.reshape(w_qkv.shape),
        own_outward.T,
        own_widen,
        own_narrow.T,
        own_small[vec_rows + 1, :n_qvb].reshape(qv_bias.shape),
        own_small[vec_rows, :n_fc1b].reshape(fc1_bias.shape),
        own_small[:vec_rows, :owned_rows],
    )
    params = (w_qkv, w_out, w_fc1, w_fc2, qv_bias, fc1_bias, norm_vec)
    moments = (mom_qkv, mom_out, mom_fc1, mom_fc2, mom_qvb, mom_fc1b, mom_vec)
    stepped = [adamw(param, grad, moment) for param, grad, moment in zip(params, owned, moments)]
    return (
        (block_output, input_grad)
        + tuple(owned)
        + tuple((entry[0] for entry in stepped))
        + tuple((entry[1] for entry in stepped))
    )


def fused(fsdp, tensor, dims, args):
    images, seqlen, width, owned, feat, hidden, c_fc, c_qv = dims
    low, f32 = jnp.bfloat16, jnp.float32
    far_n, across_n = fsdp // 2, tensor // 2
    heads = feat // HD
    padded = -(-seqlen // 16) * 16
    rows = images * padded
    vec_rows, r_fc = args[6].shape[0], args[7].shape[1]
    fc_row = -(-vec_rows // 8) * 8
    qv_row = fc_row + -(-c_fc // 8) * 8
    small_rows = -(-(qv_row + 2 * heads) // 16) * 16
    lanes = -(-max(owned, r_fc, c_qv) // 128) * 128
    half = width // 2
    part = owned // 2
    wide = 3 * feat + HD
    combined = 4 * feat
    share = 1.0 / tensor

    def kernel(
        x_in, gy_in, wq_ref, wo_ref, w1_ref, w2_ref, nv_ref, fb_ref, qb_ref, live_ref,
        own_g, own_1, own_2, out_ref, in_ref, tot_ref,
        x_ref, gy_ref, gg, g1, g2, gs, vec, bias, n1, r1, h1, qs, ks, vs, ps, os, x1, n2, r2, h2, slope, us, gfb,
        gx, gxb, gqkv, t_in, t_core, t_half, t_across, t_out,
        rs_in, rs_near, rs_sum, rs_far, sm,
        bsem_s, bsem_r, ysem_s, ysem_r, tsem_s, tsem_r, rsem_s, rsem_r, ssem_s, ssem_r,
    ):
        mine = lax.axis_index("fsdp")
        lane = lax.axis_index("tensor")
        far, near = lax.div(mine, 2), lax.rem(mine, 2)
        across, core = lax.div(lane, 2), lax.rem(lane, 2)
        twin = (2 * far + (1 - near), lane)
        mate = (mine, 2 * across + (1 - core))

        def ahead(step):
            return lax.rem(far + step, far_n)

        def behind(step):
            return lax.rem(far + far_n - step, far_n)

        def other_x(step):
            return (mine, 2 * lax.rem(across + step, across_n) + core)

        barrier = pltpu.get_barrier_semaphore()
        peers = [twin, mate]
        peers += [(2 * ahead(j) + near, lane) for j in range(1, far_n)]
        peers += [other_x(j) for j in range(1, across_n)]
        for who in peers:
            pl.semaphore_signal(barrier, inc=1, device_id=who, device_id_type=MESH_ID)

        def copy(src, dst, send, recv, target):
            return pltpu.make_async_remote_copy(
                src_ref=src, dst_ref=dst, send_sem=send, recv_sem=recv,
                device_id=target, device_id_type=MESH_ID,
            )

        pending = []

        def begin(entry):
            entry.start()
            pending.append(entry)

        gs[mine] = jnp.zeros(gs.shape[1:], low)
        gs[mine, :vec_rows, :owned] = nv_ref[...].astype(low)
        gs[mine, fc_row : fc_row + c_fc, : fb_ref.shape[1]] = fb_ref[...].astype(low)
        for h in range(heads):
            at = qv_row + 2 * h
            gs[mine, at : at + 2, :c_qv] = qb_ref[h].astype(low)
        out_t = wo_ref[...].T.astype(low)
        gg[mine] = jnp.concatenate(
            [wq_ref[0].astype(low), wq_ref[1].astype(low), wq_ref[2].astype(low), out_t], axis=1
        )
        g1[mine] = w1_ref[...].astype(low)
        g2[mine] = w2_ref[...].astype(low)
        pl.semaphore_wait(barrier, len(peers))

        units = [(gs, None)]
        for ref in (gg, g1, g2):
            units += [(ref, 0), (ref, 1)]

        def place(u, slot):
            ref, piece = units[u]
            if piece is None:
                return ref.at[slot]
            return ref.at[slot, pl.ds(piece * part, part)]

        def ring(u, s):
            slot = place(u, 2 * behind(s - 1) + near)
            return copy(slot, slot, bsem_s.at[u, s], bsem_r.at[u, s], (2 * ahead(1) + near, lane))

        def ring_wait(u, s):
            slot = place(u, 2 * behind(s) + near)
            copy(slot, slot, bsem_s.at[u, s], bsem_r.at[u, s], (2 * ahead(1) + near, lane)).wait_recv()

        def cross(u, s):
            slot = place(u, 2 * behind(s) + near)
            return copy(slot, slot, ysem_s.at[u, s], ysem_r.at[u, s], twin)

        def cross_wait(u):
            for s in range(far_n):
                slot = place(u, 2 * behind(s) + (1 - near))
                copy(slot, slot, ysem_s.at[u, s], ysem_r.at[u, s], twin).wait_recv()

        groups = [(0, 1, 2), (3, 4), (5, 6)]

        def gather():
            for u in groups[0]:
                begin(ring(u, 1))
                begin(cross(u, 0))
            for index, group in enumerate(groups):
                after = groups[index + 1] if index + 1 < len(groups) else ()
                for s in range(1, far_n):
                    for u in group:
                        yield
                        ring_wait(u, s)
                        if s + 1 < far_n:
                            begin(ring(u, s + 1))
                        begin(cross(u, s))
                    if s == 1:
                        for u in after:
                            begin(ring(u, 1))
                for u in after:
                    begin(cross(u, 0))

        flow = gather()

        def step(count=1):
            for _ in range(count):
                next(flow, None)

        step(1)

        alive = [live_ref[i].astype(f32) for i in range(images)]
        for i in range(images):
            fill = jnp.zeros((padded - seqlen, width), low)
            xi = x_in[:, i, :].astype(f32)
            x_ref[i, :seqlen] = xi.astype(low)
            x_ref[i, seqlen:] = fill
            gi = gy_in[:, i, :].astype(f32) * alive[i]
            gy_ref[i, :seqlen] = gi.astype(low)
            gy_ref[i, seqlen:] = fill
        for i in range(images):
            xf = x_ref[i].astype(f32)
            center = xf - jnp.mean(xf, axis=-1, keepdims=True)
            scale = lax.rsqrt(jnp.mean(center * center, axis=-1, keepdims=True) + epsilon)
            n1[i] = center * scale
            r1[i] = scale
        per_group = 3 * (far_n - 1)
        step(per_group)
        cross_wait(0)

        def spread(d, carry):
            rows_d = gs[d]
            source = lax.broadcasted_iota(jnp.int32, (lanes, width), 0)
            target = lax.broadcasted_iota(jnp.int32, (lanes, width), 1)
            pick = ((target == d * owned + source) & (source < owned)).astype(f32).astype(low)
            first = jnp.dot(rows_d, pick, preferred_element_type=f32)
            source = lax.broadcasted_iota(jnp.int32, (lanes, hidden), 0)
            target = lax.broadcasted_iota(jnp.int32, (lanes, hidden), 1)
            pick = (lax.div(target, HD) == source).astype(f32).astype(low)
            second = jnp.dot(rows_d, pick, preferred_element_type=f32)
            row = lax.broadcasted_iota(jnp.int32, (small_rows, hidden), 0) - fc_row
            target = lax.broadcasted_iota(jnp.int32, (small_rows, hidden), 1)
            keep = (row >= 0) & (row < c_fc) & (lax.rem(target, HD) == d * c_fc + row)
            second = jnp.sum(jnp.where(keep, second, 0.0), axis=0, keepdims=True)
            source = lax.broadcasted_iota(jnp.int32, (lanes, wide), 0)
            target = lax.broadcasted_iota(jnp.int32, (lanes, wide), 1)
            pick = ((lax.rem(target, HD) == d * c_qv + source) & (source < c_qv)).astype(f32)
            third = jnp.dot(rows_d, pick.astype(low), preferred_element_type=f32)
            row = lax.broadcasted_iota(jnp.int32, (small_rows, wide), 0) - qv_row
            target = lax.broadcasted_iota(jnp.int32, (small_rows, wide), 1)
            group = lax.rem(row, 2) * (2 * heads) + lax.div(row, 2)
            keep = (row >= 0) & (row < 2 * heads) & (lax.div(target, HD) == group)
            third = jnp.sum(jnp.where(keep, third, 0.0), axis=0, keepdims=True)
            return (carry[0] + first, carry[1] + second, carry[2] + third)

        start = (
            jnp.zeros((small_rows, width), f32),
            jnp.zeros((1, hidden), f32),
            jnp.zeros((1, wide), f32),
        )
        spread_v, bias_f, spread_q = lax.fori_loop(0, fsdp, spread, start)
        vec[...] = spread_v
        gain1, shift1, gain2, shift2, bias_o, bias_2 = (vec[r : r + 1] for r in range(6))
        bias[...] = spread_q
        for i in range(images):
            h1[i] = (n1[i] * gain1 + shift1).astype(low)
        cross_wait(1)
        cross_wait(2)

        def flat(ref):
            return ref[...].reshape(ref.shape[0] * ref.shape[1], ref.shape[2])

        def cols(ref, start, size):
            piece = ref[:, :, start : start + size]
            return piece.reshape(ref.shape[0] * ref.shape[1], size)

        span = feat + HD
        k_at, v_at, o_at = feat - HD, 2 * feat, combined - span
        head_of = lax.broadcasted_iota(jnp.int32, (padded, span), 1) // HD
        key_at = lax.broadcasted_iota(jnp.int32, (padded, padded), 1)

        def nn(a, b):
            return jnp.dot(a, b, preferred_element_type=f32)

        def nt(a, b):
            return lax.dot_general(a, b, (((1,), (1,)), ((), ())), preferred_element_type=f32)

        def tn(a, b):
            return lax.dot_general(a, b, (((0,), (0,)), ((), ())), preferred_element_type=f32)

        mine_half = pl.ds(pl.multiple_of(core * half, half), half)
        mate_half = pl.ds(pl.multiple_of((1 - core) * half, half), half)

        def total(k, i):
            def sem(ref, index):
                return ref.at[k, i, index]

            first = copy(t_in.at[k, i, :, mate_half], t_core.at[k, i], sem(tsem_s, 0),
                         sem(tsem_r, 0), mate)
            begin(first)
            yield
            first.wait_recv()
            mine_sum = t_in[k, i, :, mine_half].astype(f32) + t_core[k, i].astype(f32)
            t_half[k, i] = mine_sum.astype(low)
            hops = []
            for j in range(1, across_n):
                hops.append(copy(t_half.at[k, i], t_across.at[k, i, j - 1], sem(tsem_s, 1 + j),
                                 sem(tsem_r, 1 + j), other_x(j)))
                begin(hops[-1])
            yield
            summed = t_half[k, i].astype(f32)
            for j in range(1, across_n):
                hops[j - 1].wait_recv()
                summed = summed + t_across[k, i, j - 1].astype(f32)
            t_out[k, i, :, mine_half] = summed.astype(low)
            own = t_out.at[k, i, :, mine_half]
            begin(copy(own, own, sem(tsem_s, 1), sem(tsem_r, 1), mate))
            yield
            theirs = t_out.at[k, i, :, mate_half]
            copy(theirs, theirs, sem(tsem_s, 1), sem(tsem_r, 1), mate).wait_recv()
            yield

        sums = {}

        def project(i):
            pr = nn(h1[i], cols(gg, 0, wide)) + bias[...]
            qs[i] = pltpu.roll(pr[:, :span], HD, 1).astype(low)
            ks[i] = pr[:, k_at : k_at + span].astype(low)
            vs[i] = pr[:, v_at : v_at + span].astype(low)

        def attend_head(i, h, mixed):
            q_h = jnp.where(head_of == h + 1, qs[i], jnp.zeros_like(qs[i]))
            s = nt(q_h, ks[i]) * 0.125
            s = jnp.where(key_at < seqlen, s, -1e30)
            e = jnp.exp(s - jnp.max(s, axis=-1, keepdims=True))
            p = e * (1.0 / jnp.sum(e, axis=-1, keepdims=True))
            ps[i, h] = p
            o_h = nn(p.astype(low), vs[i])
            return jnp.where(head_of == h, o_h, mixed)

        attn = []
        for i in range(images):
            project(i)
            step(1)
            mixed = jnp.zeros((padded, span), f32)
            for h in range(heads):
                mixed = attend_head(i, h, mixed)
                step(1)
                for entry in attn:
                    if h < 2:
                        next(entry)
            os[i] = pltpu.roll(mixed, HD, 1).astype(low)
            t_in[0, i] = nt(os[i], cols(gg, o_at, span)).astype(low)
            attn.append(total(0, i))
            next(attn[i])
            step(1)
        step(2)
        next(attn[0], None) if images > 1 and heads < 2 else None
        next(attn[-1])
        gy_sum = None
        for i in range(images):
            add = jnp.sum(gy_ref[i].astype(f32), axis=0, keepdims=True)
            gy_sum = add if gy_sum is None else gy_sum + add
        step(1)
        for entry in attn:
            for _ in entry:
                pass
        step(100)

        for i in range(images):
            res = x_ref[i].astype(f32) + t_out[0, i].astype(f32) + bias_o
            x1[i] = res
            center = res - jnp.mean(res, axis=-1, keepdims=True)
            scale = lax.rsqrt(jnp.mean(center * center, axis=-1, keepdims=True) + epsilon)
            unit = center * scale
            n2[i] = unit
            r2[i] = scale
            h2[i] = (unit * gain2 + shift2).astype(low)
        cross_wait(3)
        cross_wait(4)
        for i in range(images):
            f = nn(h2[i], flat(g1)) + bias_f
            phi = 0.5 * (1.0 + lax.erf(f * sqrt_half))
            us[i] = (f * phi).astype(low)
            slope[i] = phi + f * jnp.exp(-0.5 * f * f) * inv_root
        onward = tuple(range(1, far_n))

        def scatter_y(p, steps):
            for j in steps:
                begin(copy(rs_in.at[p, 2 * ahead(j) + (1 - near)], rs_near.at[p, j],
                           rsem_s.at[p, j], rsem_r.at[p, j], twin))

        def scatter_z(p, j):
            block = rs_in.at[p, 2 * ahead(j) + (1 - near)]
            copy(block, rs_near.at[p, j], rsem_s.at[p, j], rsem_r.at[p, j], twin).wait_recv()
            rs_sum[p, j - 1] = (
                rs_in[p, 2 * ahead(j) + near].astype(f32) + rs_near[p, j].astype(f32)
            ).astype(low)
            begin(copy(rs_sum.at[p, j - 1], rs_far.at[p, j - 1], rsem_s.at[p, far_n + j],
                       rsem_r.at[p, far_n + j], (2 * ahead(j) + near, lane)))

        def scatter_end(p, ref):
            block = rs_in.at[p, 2 * far + (1 - near)]
            copy(block, rs_near.at[p, 0], rsem_s.at[p, 0], rsem_r.at[p, 0], twin).wait_recv()
            acc = rs_in[p, mine].astype(f32) + rs_near[p, 0].astype(f32)
            for j in range(1, far_n):
                copy(rs_sum.at[p, j - 1], rs_far.at[p, j - 1], rsem_s.at[p, far_n + j],
                     rsem_r.at[p, far_n + j], (2 * ahead(j) + near, lane)).wait_recv()
                acc = acc + rs_far[p, j - 1].astype(f32)
            ref[...] = acc

        def blocks(grad):
            return grad.astype(low).reshape(fsdp, owned, grad.shape[1])

        rs_in[0] = blocks(tn(flat(gy_ref), flat(us)))
        cross_wait(5)
        scatter_y(0, onward)
        cross_wait(6)
        two, mlp = [], []
        gf_sum = None
        row2 = row3 = None

        def plus(a, b):
            return b if a is None else a + b

        for i in range(images):
            gf = nn(gy_ref[i], flat(g2)) * slope[i]
            gfb[i] = gf.astype(low)
            gf_sum = plus(gf_sum, jnp.sum(gf, axis=0, keepdims=True))
            t_in[1, i] = nt(gfb[i], flat(g1)).astype(low)
            two.append(total(1, i))
            next(two[i])

        for i in range(images):
            next(two[i])
        rs_in[1] = blocks(tn(flat(h2), flat(gfb)))
        scatter_y(1, onward)
        for i in range(images):
            t_in[2, i] = nt(us[i], flat(g2)).astype(low)
        for i in range(images):
            term = t_in[1, i].astype(f32)
            row2 = plus(row2, jnp.sum(term * n2[i], axis=0, keepdims=True))
            row3 = plus(row3, jnp.sum(term, axis=0, keepdims=True))
        for i in range(images):
            next(two[i])
        for i in range(images):
            mlp.append(total(2, i))
            next(mlp[i])
        for i in range(images):
            next(two[i])
            next(mlp[i])

        events = [(p, j) for p in range(2) for j in range(1, far_n)]

        def reduce_step():
            if events:
                scatter_z(*events.pop(0))

        gx_sum = row7 = row0 = row1 = None
        one = []
        for i in range(images):
            e = t_out[1, i].astype(f32) * gain2
            unit = n2[i]
            g = gy_ref[i].astype(f32) + r2[i] * (
                e
                - jnp.mean(e, axis=-1, keepdims=True)
                - unit * jnp.mean(e * unit, axis=-1, keepdims=True)
            )
            gx[i] = g
            gxb[i] = g.astype(low)
            gx_sum = plus(gx_sum, jnp.sum(g, axis=0, keepdims=True))
            go = nn(gxb[i], cols(gg, o_at, span))
            go = pltpu.roll(go, span - HD, 1).astype(low)
            dq = jnp.zeros((padded, span), f32)
            dk = jnp.zeros((padded, span), f32)
            dv = jnp.zeros((padded, span), f32)
            for h in range(heads):
                go_h = jnp.where(head_of == h, go, jnp.zeros_like(go))
                p = ps[i, h]
                gp = nt(go_h, vs[i])
                gs_h = (p * (gp - jnp.sum(p * gp, axis=-1, keepdims=True))).astype(low)
                dq = jnp.where(head_of == h + 1, nn(gs_h, ks[i]), dq)
                dk = jnp.where(head_of == h + 1, tn(gs_h, qs[i]), dk)
                dv = jnp.where(head_of == h, tn(p.astype(low), go), dv)
                reduce_step()
            dq = pltpu.roll(dq, span - HD, 1) * 0.125
            dk = dk * 0.125
            edge = 2 * HD
            pieces = jnp.concatenate(
                [dq[:, :edge], dq[:, edge:] + dk[:, :edge], dk[:, edge:], dv], axis=1
            )
            gqkv[i] = pieces.astype(low)
            row7 = plus(row7, jnp.sum(pieces, axis=0, keepdims=True))
            term = nt(gqkv[i], cols(gg, 0, wide)).astype(low)
            t_in[3, i] = term
            one.append(total(3, i))
            next(one[i])
            term = term.astype(f32)
            row0 = plus(row0, jnp.sum(term * n1[i], axis=0, keepdims=True))
            row1 = plus(row1, jnp.sum(term, axis=0, keepdims=True))

        grad = tn(flat(h1), flat(gqkv))
        outer = tn(flat(gxb), flat(os))
        rs_in[2, :, :, :o_at] = blocks(grad[:, :o_at])
        tail = grad[:, o_at:]
        rs_in[2, :, :, o_at : o_at + tail.shape[1]] = blocks(
            tail + outer[:, : tail.shape[1]]
        )
        rs_in[2, :, :, o_at + tail.shape[1] :] = blocks(outer[:, tail.shape[1] :])

        mine_rows = sm.at[0]
        sm[0, 0:1] = row0
        sm[0, 1:2] = row1
        sm[0, 2:3] = row2
        sm[0, 3:4] = row3
        sm[0, 4:5] = gx_sum * share
        sm[0, 5:6] = gy_sum * share
        sm[0, 6:7] = gf_sum
        sm[0, 7:8] = jnp.zeros((1, width), f32)
        sm[0, 7:8, :wide] = row7
        while events:
            reduce_step()
        for i in range(images):
            next(one[i])
        scatter_y(2, onward)
        for p in range(3):
            scatter_y(p, (0,))
        shared = lax.broadcasted_iota(jnp.int32, (8, width), 0) < 6

        def small_flow():
            hop = copy(sm.at[0], sm.at[1], ssem_s.at[0], ssem_r.at[0], mate)
            begin(hop)
            yield
            hop.wait_recv()
            sm[2] = sm[0] + jnp.where(shared, sm[1], 0.0)
            hops = []
            for j in range(1, across_n):
                hops.append(copy(sm.at[2], sm.at[2 + j], ssem_s.at[j], ssem_r.at[j], other_x(j)))
                begin(hops[-1])
            yield
            summed = sm[2]
            for j in range(1, across_n):
                hops[j - 1].wait_recv()
                summed = summed + jnp.where(shared, sm[2 + j], 0.0)
            base = 2 + across_n
            sm[base] = summed
            hop = copy(sm.at[base], sm.at[base + 1], ssem_s.at[across_n], ssem_r.at[across_n], twin)
            begin(hop)
            yield
            hop.wait_recv()
            sm[base + 2] = sm[base] + sm[base + 1]
            hops = []
            for j in range(1, far_n):
                hops.append(copy(sm.at[base + 2], sm.at[base + 2 + j], ssem_s.at[across_n + j],
                                 ssem_r.at[across_n + j], (2 * ahead(j) + near, lane)))
                begin(hops[-1])
            yield
            summed = sm[base + 2]
            for j in range(1, far_n):
                hops[j - 1].wait_recv()
                summed = summed + sm[base + 2 + j]
            tot_ref[...] = summed
            yield

        tiny = small_flow()
        next(tiny)
        for entry in mlp:
            next(entry)
        next(tiny)
        for i in range(images):
            next(one[i])
        next(tiny)
        scatter_end(0, own_2)
        next(tiny)
        scatter_end(1, own_1)
        for entry in mlp:
            for _ in entry:
                pass
        for i in range(images):
            x1[i] = x1[i] + t_out[2, i].astype(f32) + bias_2
        out_ref[...] = jnp.stack(
            [x1[i, :seqlen] * alive[i] for i in range(images)], axis=1
        ).astype(low)
        for j in range(1, far_n):
            scatter_z(2, j)
        next(tiny)
        for i in range(images):
            for _ in one[i]:
                pass
            e = t_out[3, i].astype(f32) * gain1
            unit = n1[i]
            grad_in = gx[i] + r1[i] * (
                e
                - jnp.mean(e, axis=-1, keepdims=True)
                - unit * jnp.mean(e * unit, axis=-1, keepdims=True)
            )
            in_ref[:, i, :] = grad_in[:seqlen]
        scatter_end(2, own_g)
        for entry in pending:
            entry.wait_send()

    shape = jax.ShapeDtypeStruct
    outs = (
        shape((owned, combined), f32),
        shape((owned, hidden), f32),
        shape((owned, hidden), f32),
        shape((seqlen, images, width), low),
        shape((seqlen, images, width), f32),
        shape((8, width), f32),
    )
    span = feat + HD
    sp = (images, padded)

    def vm(dims, kind):
        return pltpu.VMEM(dims, kind)

    few = max(far_n - 1, 1)
    xs = max(across_n - 1, 1)
    dma = pltpu.SemaphoreType.DMA
    scratch = [
        vm(sp + (width,), low), vm(sp + (width,), low),
        vm((fsdp, owned, combined), low),
        vm((fsdp, owned, hidden), low),
        vm((fsdp, owned, hidden), low),
        vm((fsdp, small_rows, lanes), low),
        vm((small_rows, width), f32),
        vm((1, wide), f32),
        vm(sp + (width,), f32), vm(sp + (1,), f32), vm(sp + (width,), low),
        vm(sp + (span,), low), vm(sp + (span,), low), vm(sp + (span,), low),
        vm((images, heads, padded, padded), f32),
        vm(sp + (span,), low),
        vm(sp + (width,), f32),
        vm(sp + (width,), f32), vm(sp + (1,), f32), vm(sp + (width,), low),
        vm(sp + (hidden,), f32), vm(sp + (hidden,), low), vm(sp + (hidden,), low),
        vm(sp + (width,), f32), vm(sp + (width,), low), vm(sp + (wide,), low),
        vm((4,) + sp + (width,), low),
        vm((4,) + sp + (half,), low), vm((4,) + sp + (half,), low),
        vm((4, images, xs, padded, half), low),
        vm((4,) + sp + (width,), low),
        vm((3, fsdp, owned, combined), low),
        vm((3, far_n, owned, combined), low),
        vm((3, few, owned, combined), low),
        vm((3, few, owned, combined), low),
        vm((4 + across_n + far_n, 8, width), f32),
        dma((7, far_n)), dma((7, far_n)), dma((7, far_n)), dma((7, far_n)),
        dma((4, images, 1 + across_n)), dma((4, images, 1 + across_n)),
        dma((3, 2 * far_n)), dma((3, 2 * far_n)),
        dma((across_n + far_n,)), dma((across_n + far_n,)),
    ]
    space = pl.BlockSpec(memory_space=pltpu.VMEM)
    return pl.pallas_call(
        kernel,
        out_shape=outs,
        in_specs=[space] * (len(args) - 1) + [pl.BlockSpec(memory_space=pltpu.SMEM)],
        out_specs=tuple([space] * len(outs)),
        scratch_shapes=scratch,
        compiler_params=pltpu.CompilerParams(
            collective_id=1, has_side_effects=True, vmem_limit_bytes=46 * 1024 * 1024
        ),
        name="fused_layer",
    )(*args)


def update(own_g, own_1, own_2, sums, out_rows, in_rows, params, moments):
    f32 = jnp.float32
    feat = params[0].shape[2]
    owned = params[0].shape[1]
    width = sums.shape[1]
    heads, _, c_qv = params[4].shape
    c_fc, r_fc = params[5].shape
    vec_rows = params[6].shape[0]

    def kernel(*refs):
        g_ref, g1_ref, g2_ref, sum_ref = refs[:4]
        rows_in, p_in, m_in = refs[4:6], refs[6:13], refs[13:20]
        g_out, p_out, m_out, rows_out = refs[20:27], refs[27:34], refs[34:41], refs[41:43]
        sems = refs[43]
        moves = [
            pltpu.make_async_copy(rows_in[k], rows_out[k], sems.at[k]) for k in range(2)
        ]
        for move in moves:
            move.start()
        mine = lax.axis_index("fsdp")

        def advance(param, one, two, grad):
            first = 0.9 * one + 0.1 * grad
            second = 0.999 * two + 0.001 * grad * grad
            fresh = param - 0.004 * (
                first / corr_one / (jnp.sqrt(second / corr_two) + 1e-08) + 0.05 * param
            )
            return fresh, first, second

        for c in range(3):
            grad = g_ref[:, c * feat : (c + 1) * feat]
            g_out[0][c] = grad
            p_out[0][c], m_out[0][0, c], m_out[0][1, c] = advance(
                p_in[0][c], m_in[0][0, c], m_in[0][1, c], grad
            )
        for k, grad in ((1, g_ref[:, 3 * feat :].T), (2, g1_ref[...]), (3, g2_ref[...])):
            g_out[k][...] = grad
            p_out[k][...], m_out[k][0], m_out[k][1] = advance(
                p_in[k][...], m_in[k][0], m_in[k][1], grad
            )

        def pick(rows, cols, values, row_of_lane, lane_base, step):
            count = values.shape[1]
            lane = lax.broadcasted_iota(jnp.int32, (rows, count), 1)
            mask = row_of_lane(lane, lax.broadcasted_iota(jnp.int32, (rows, count), 0))
            spread = jnp.where(mask, jnp.broadcast_to(values, (rows, count)), 0.0)
            lane = lax.broadcasted_iota(jnp.int32, (count, 128), 0)
            place = lax.broadcasted_iota(jnp.int32, (count, 128), 1)
            chosen = (step(lane, place)).astype(f32)
            return jnp.dot(
                spread, chosen, precision=lax.Precision.HIGHEST, preferred_element_type=f32
            )

        hidden = sum_ref[vec_rows : vec_rows + 1]
        grad = pick(
            c_fc, r_fc, hidden,
            lambda l, r: lax.rem(l, HD) == mine * c_fc + r, None,
            lambda l, p: lax.div(l, HD) == p,
        )[:, :r_fc]
        g_out[5][...] = grad
        p_out[5][...], m_out[5][0], m_out[5][1] = advance(
            p_in[5][...], m_in[5][0], m_in[5][1], grad
        )
        triple = sum_ref[vec_rows + 1 : vec_rows + 2]
        grads = pick(
            8, c_qv, triple,
            lambda l, r: lax.div(l, HD) == lax.rem(r, 2) * (2 * heads) + lax.div(r, 2), None,
            lambda l, p: (lax.rem(l, HD) == mine * c_qv + p) & (p < c_qv),
        )
        for h in range(heads):
            grad = grads[2 * h : 2 * h + 2, :c_qv]
            g_out[4][h] = grad
            p_out[4][h], m_out[4][0, h], m_out[4][1, h] = advance(
                p_in[4][h], m_in[4][0, h], m_in[4][1, h], grad
            )
        lane = lax.broadcasted_iota(jnp.int32, (width, 128), 0)
        place = lax.broadcasted_iota(jnp.int32, (width, 128), 1)
        chosen = ((lane == mine * owned + place) & (place < owned)).astype(f32)
        grad = jnp.dot(
            sum_ref[...], chosen, precision=lax.Precision.HIGHEST, preferred_element_type=f32
        )[:vec_rows, :owned]
        g_out[6][...] = grad
        p_out[6][...], one, two = advance(p_in[6][...], m_in[6][:, 0], m_in[6][:, 1], grad)
        m_out[6][:, 0] = one
        m_out[6][:, 1] = two
        for move in moves:
            move.wait()

    shape = jax.ShapeDtypeStruct
    outs = [shape(p.shape, f32) for p in params] * 2 + [shape(m.shape, f32) for m in moments]
    outs += [shape(a.shape, a.dtype) for a in (out_rows, in_rows)]
    space = pl.BlockSpec(memory_space=pltpu.VMEM)
    spaces = [space] * 21 + [pl.BlockSpec(memory_space=pl.ANY)] * 2
    result = pl.pallas_call(
        kernel,
        out_shape=tuple(outs),
        in_specs=[space] * 20,
        out_specs=tuple(spaces),
        scratch_shapes=[pltpu.SemaphoreType.DMA((2,))],
        compiler_params=pltpu.CompilerParams(vmem_limit_bytes=24 * 1024 * 1024),
        name="update",
    )(own_g, own_1, own_2, sums, out_rows, in_rows, *params, *moments)
    return result[:7], result[7:14], result[14:21], result[21:]


def on_device(fsdp, tensor, *args):
    owned = args[3].shape[0]
    local = args[3].shape[2]
    fits = (
        owned % 16 == 0
        and (local + HD) % 128 == 0
        and 4 * local == args[0].shape[2] == args[5].shape[1]
        and fsdp % 2 == 0
        and fsdp <= 16
    )
    return (fused_step if fits else plain_step)(fsdp, tensor, *args)


def fused_step(
    fsdp, tensor, block_input, output_grad, live_images, w_qkv, w_out, w_fc1, w_fc2, qv_bias,
    fc1_bias, norm_vec, mom_qkv, mom_out, mom_fc1, mom_fc2, mom_qvb, mom_fc1b, mom_vec,
):
    images, seqlen, width = block_input.shape
    owned, _, feat = w_qkv.shape
    hidden = w_fc1.shape[1]
    x_t, gy_t = block_input.transpose(1, 0, 2), output_grad.transpose(1, 0, 2)
    nv, fb, qb = norm_vec, fc1_bias.T, qv_bias.transpose(1, 0, 2)
    dims = (images, seqlen, width, owned, feat, hidden, fc1_bias.shape[1], qv_bias.shape[2])
    wq, w2 = w_qkv.transpose(1, 0, 2), w_fc2.T
    own_g, own_1, own_2, out_rows, in_rows, sums = fused(
        fsdp, tensor, dims, (x_t, gy_t, wq, w_out, w_fc1, w2, nv, fb, qb, live_images)
    )
    grads, news, moms, flows = update(
        own_g, own_1, own_2, sums, out_rows, in_rows,
        (wq, w_out, w_fc1, w2, qb, fb, nv),
        (
            mom_qkv.transpose(0, 2, 1, 3), mom_out, mom_fc1, mom_fc2.transpose(0, 2, 1),
            mom_qvb.transpose(0, 2, 1, 3), mom_fc1b.transpose(0, 2, 1), mom_vec.transpose(1, 0, 2),
        ),
    )

    def back(a):
        return (
            a[0].transpose(1, 0, 2), a[1], a[2], a[3].T, a[4].transpose(1, 0, 2), a[5].T, a[6],
        )

    return (
        tuple(a.transpose(1, 0, 2) for a in flows) + back(grads) + back(news)
        + (
            moms[0].transpose(0, 2, 1, 3), moms[1], moms[2], moms[3].transpose(0, 2, 1),
            moms[4].transpose(0, 2, 1, 3), moms[5].transpose(0, 2, 1), moms[6].transpose(1, 0, 2),
        )
    )


def solution(mesh):
    return jax.shard_map(
        functools.partial(on_device, mesh.shape["fsdp"], mesh.shape["tensor"]),
        mesh=mesh,
        in_specs=(
            P("fsdp", None, None),
            P("fsdp", None, None),
            P("fsdp"),
            P("fsdp", None, "tensor"),
            P("tensor", "fsdp"),
            P("fsdp", "tensor"),
            P("tensor", "fsdp"),
            P(None, "tensor", "fsdp"),
            P("tensor", "fsdp"),
            P(None, "fsdp"),
            P(None, "fsdp", None, "tensor"),
            P(None, "tensor", "fsdp"),
            P(None, "fsdp", "tensor"),
            P(None, "tensor", "fsdp"),
            P(None, None, "tensor", "fsdp"),
            P(None, "tensor", "fsdp"),
            P(None, None, "fsdp"),
        ),
        out_specs=(
            P("fsdp", None, None),
            P("fsdp", None, None),
            P("fsdp", None, "tensor"),
            P("tensor", "fsdp"),
            P("fsdp", "tensor"),
            P("tensor", "fsdp"),
            P(None, "tensor", "fsdp"),
            P("tensor", "fsdp"),
            P(None, "fsdp"),
            P("fsdp", None, "tensor"),
            P("tensor", "fsdp"),
            P("fsdp", "tensor"),
            P("tensor", "fsdp"),
            P(None, "tensor", "fsdp"),
            P("tensor", "fsdp"),
            P(None, "fsdp"),
            P(None, "fsdp", None, "tensor"),
            P(None, "tensor", "fsdp"),
            P(None, "fsdp", "tensor"),
            P(None, "tensor", "fsdp"),
            P(None, None, "tensor", "fsdp"),
            P(None, "tensor", "fsdp"),
            P(None, None, "fsdp"),
        ),
        check_vma=False,
    )
```
